32 devices in a mesh: wide: 8 (over z, y), narrow: 4 (over x, core).
Axes of the slice: x: 2, y: 2, z: 4, core: 2. Of those that a mesh axis runs over, the one named last changes fastest.
Arguments:
- op_blocks: bfloat16 [512, 6, 192, 192], P('wide', None, 'narrow'), may hold values from -6 to 6
- prolong: bfloat16 [512, 9216], P('wide', 'narrow'), may hold values from -0.4375 to 0.4375
- col_index: int32 [512, 6], P('wide'), may hold values from 0 to 511, as said below
- slot_index: int32 [512, 6], P('wide'), may hold values from 0 to 7
- dest_owner: int32 [512, 1], P('wide'), may hold values from 0 to 7; in each aligned block of 64 rows (0 to 63, 64 to 127, ...) at most 16 rows name the same one
- dest_local: int32 [512], P('wide'), may hold values from 0 to 15
Outputs:
- coarse: float32 [128, 48, 384], P('wide', 'narrow')
The draws below stay inside these ranges and needn't reach their ends.
Inputs may be any that keep to these rules, and one draw needn't show every extreme that they name: `col_index`: the first column of each row is the row itself; every column lies in the block rows of the same wide index or of the one just before or after it. `dest_owner`: among the 64 rows of one wide index no owner is named more than 16 times; some owner is named exactly 16 times.
All inputs are finite; a program needn't handle non-finite values.
Results may differ from the reference program's by a relative error of at most 0.0029.
Values may be sent and summed in bfloat16 or wider, within the bound.
A program may use at most 128 MiB of HBM per device.

```python
import math
import jax
import jax.numpy as jnp
import numpy as np
from jax import lax

B = 192
M = 48
K = 6
KC = 8
RB_DEV = 64
AGG_DEV = 16
CAP = 16
NFINE = 512
N_WIDE = 8


def draw_col_index(key, part):
    rows = jnp.arange(NFINE, dtype=jnp.int32)
    start = rows // RB_DEV * RB_DEV
    offsets = jax.random.randint(key, (NFINE, K), -RB_DEV, 2 * RB_DEV, dtype=jnp.int32)
    columns = start[:, None] + offsets
    columns = jnp.where(columns < 0, columns + RB_DEV, columns)
    columns = jnp.where(columns >= NFINE, columns - RB_DEV, columns)
    first = jnp.arange(K, dtype=jnp.int32)[None, :] == 0
    return jnp.where(first, rows[:, None], columns).astype(jnp.int32)


def with_ends(values, key, smallest, high):
    index_at = [jax.random.randint(jax.random.fold_in(key, axis), (), 0, length) for axis, length in enumerate(values.shape)]
    main_axis = values.shape.index(max(values.shape))
    neighbour = index_at[:main_axis] + [(index_at[main_axis] + 1) % values.shape[main_axis]] + index_at[main_axis + 1:]
    return values.at[tuple(index_at)].set(smallest).at[tuple(neighbour)].set(high)


def block_levels(key, dims, cuts, least, largest):
    def one(axis_at, blocks):
        heights = jax.random.uniform(jax.random.fold_in(jax.random.fold_in(key, 6), axis_at), (blocks,), jnp.float32, least / len(cuts), largest / len(cuts))
        return jnp.repeat(jnp.exp(heights), dims[axis_at] // blocks).reshape((-1,) + (1,) * (len(dims) - axis_at - 1))

    level = one(*cuts[0])
    for cut in cuts[1:]:
        level = level * one(*cut)
    return level


def shared_out(stream_key, own, number, rows, count, top, bound, slope):
    ranking = jax.random.permutation(stream_key, count)
    packed, common = shares(count, rows * top, bound, slope, True), shares(count, rows * top, bound, slope, False)
    places = jnp.arange(count)

    def named(tallies, turn):
        used = int((tallies > 0).sum())
        fixed = max(1, used // 4)
        shifted = fixed + (places - fixed + turn * (used - fixed)) % max(1, count - fixed)
        return jnp.zeros((count,), jnp.int32).at[ranking[jnp.where(places < fixed, places, shifted)]].set(jnp.asarray(tallies, jnp.int32))

    tallies = jnp.where(number % 4 == 0, named(packed, number // 4), named(common, number - number // 4 - 1))
    mixed = jax.random.permutation(jax.random.fold_in(own, 3), count)
    donor, sink = mixed[0:count // 2 * 2:2], mixed[1:count // 2 * 2:2]
    slack = jnp.minimum(tallies[donor] - 1, bound - tallies[sink]) // 2
    slack = jnp.where((donor == ranking[0]) | (sink == ranking[0]) | (tallies[sink] == 0), 0, jnp.maximum(slack, 0))
    shifted = jax.random.randint(jax.random.fold_in(own, 4), (count // 2,), 0, 1 << 20) % (slack + 1)
    tallies = tallies.at[donor].add(-shifted).at[sink].add(shifted)
    items = jnp.searchsorted(jnp.cumsum(tallies), jnp.arange(rows * top), side="right").astype(jnp.int32)
    grid = items.reshape(top, rows).T
    grid = grid[jax.random.permutation(jax.random.fold_in(own, 1), rows)]
    turn = jax.random.randint(jax.random.fold_in(own, 2), (rows, 1), 0, top)
    return jnp.take_along_axis(grid, (jnp.arange(top)[None, :] + turn) % top, axis=1)


def shares(number_of, total, most, skew, full):
    portions = [(1 << 20) // math.isqrt(grade ** skew) + 1 for grade in range(1, number_of + 1)]
    largest = most if full else min(most, max(-(-total // number_of), total * portions[0] // sum(portions)))
    least = 1 if total - largest >= number_of - 1 else 0
    counts, rest = [largest] + [least] * (number_of - 1), total - largest - least * (number_of - 1)
    while rest > 0:
        candidates = [i for i in range(1, number_of) if counts[i] < largest] or [i for i in range(1, number_of) if counts[i] < most]
        mass, left = sum([portions[i] for i in candidates]), rest
        for i in candidates:
            extra = min(most - counts[i], max(1, left * portions[i] // mass), rest)
            counts[i] = counts[i] + extra
            rest = rest - extra
    return np.array(counts)


def gaussian(stream_key, dims, width, bound, shards=(), kind=jnp.bfloat16):
    factor_of = block_levels(stream_key, dims, shards, -0.22, 0.18) if shards else 1.0
    entries = jax.random.normal(stream_key, dims, jnp.float32) * width * factor_of
    return jnp.minimum(jnp.maximum(entries, -bound), bound).astype(kind)


def setup_inputs(seed: int = 0) -> dict:
    arg_keys = jax.random.split(jax.random.key(seed), 7)
    op_blocks = gaussian(arg_keys[0], (NFINE, K, B, B), 1.0, 6.0, ((0, 8), (2, 4)))
    prolong = gaussian(arg_keys[1], (NFINE, B * M), B ** -0.5, 0.4375, ((0, 8), (1, 4)))
    col_index = draw_col_index(jax.random.fold_in(arg_keys[6], 71), 0)
    slot_index = with_ends(jax.random.randint(arg_keys[3], (NFINE, K), 0, KC), jax.random.fold_in(arg_keys[3], 1), 0, KC - 1).astype(jnp.int32)
    dest_owner_keys = jax.random.split(jax.random.fold_in(arg_keys[4], 1), NFINE // RB_DEV)
    dest_owner_turns = jax.random.permutation(jax.random.fold_in(arg_keys[4], 3), NFINE // RB_DEV)
    dest_owner = jax.vmap(lambda own, number: shared_out(jax.random.fold_in(arg_keys[4], 2), own, number, RB_DEV, N_WIDE, 1, CAP, 2))(dest_owner_keys, dest_owner_turns).reshape((NFINE, 1))
    dest_local = with_ends(jax.random.randint(arg_keys[5], (NFINE,), 0, AGG_DEV), jax.random.fold_in(arg_keys[5], 1), 0, AGG_DEV - 1).astype(jnp.int32)
    return {"op_blocks": op_blocks, "prolong": prolong, "col_index": col_index, "slot_index": slot_index, "dest_owner": dest_owner, "dest_local": dest_local}


def reference(op_blocks, prolong, col_index, slot_index, dest_owner, dest_local):
    fine_count = op_blocks.shape[0]
    prolong_blocks = prolong.reshape(fine_count, B, M)
    agg = (dest_owner[:, 0] * AGG_DEV + dest_local).astype(jnp.int32)

    def galerkin_row(pieces):
        op_row, columns, slot_row, own_block = pieces
        gathered = jnp.take(prolong_blocks, columns, axis=0)
        applied = jnp.einsum('krb,kbm->krm', op_row.astype(jnp.float32), gathered.astype(jnp.float32),
                             precision=lax.Precision.HIGHEST).astype(jnp.bfloat16)
        projected = jnp.einsum('rc,krm->kcm', own_block.astype(jnp.float32), applied.astype(jnp.float32),
                               precision=lax.Precision.HIGHEST)
        selector = (slot_row[:, None] == jnp.arange(KC, dtype=jnp.int32)[None, :]).astype(jnp.float32)
        summed = jnp.einsum('ks,kcm->csm', selector, projected, precision=lax.Precision.HIGHEST)
        return summed.reshape(M, KC * M)

    rows_all = lax.map(galerkin_row, (op_blocks, col_index, slot_index, prolong_blocks))
    return jax.ops.segment_sum(rows_all, agg, num_segments=AGG_DEV * N_WIDE)
```

```python
import functools

import jax
import jax.numpy as jnp
from jax import lax
from jax.experimental import pallas as pl
from jax.experimental.pallas import tpu as pltpu
from jax.sharding import PartitionSpec as P

B = 192
M = 48
KC = 8
AGG_DEV = 16
HALF = 64
QUAD = 4
MESH = pl.DeviceIdType.MESH
F32 = jnp.float32
BF16 = jnp.bfloat16
I32 = jnp.int32


def padded(cells, axis):
    count = lax.axis_size(axis)
    ends = count - 1
    return jnp.concatenate(
        [
            lax.ppermute(cells, axis, [(i, (i + 1) % count) for i in range(ends)]),
            cells,
            lax.ppermute(cells, axis, [((i + 1) % count, i) for i in range(ends)]),
        ],
        axis=0,
    )


def product_kernel(terms, parts, col_ref, slot_ref, op_ref, near_ref, own_ref, out_ref, acc):
    step = pl.program_id(0)
    side = M // parts
    lane_half = lax.broadcasted_iota(I32, (M, 2 * HALF), 1) // HALF
    rows = []
    for j in range(QUAD):
        base = (step * QUAD + j) * terms
        acc[j] = jnp.zeros_like(acc[j])
        applied = [
            jnp.dot(op_ref[j, k], near_ref[col_ref[base + k]], preferred_element_type=F32).astype(BF16)
            for k in range(terms)
        ]
        projected = jnp.dot(own_ref[j], jnp.concatenate(applied, axis=1), preferred_element_type=F32)
        for k in range(terms):
            slot = slot_ref[base + k]
            piece = projected[:, k * 2 * HALF : (k + 1) * 2 * HALF]
            acc[j, slot // 2] += jnp.where(lane_half == slot % 2, piece, 0.0)
        rows.append(
            jnp.concatenate(
                [acc[j, s // 2][:, (s % 2) * HALF : (s % 2) * HALF + M] for s in range(KC)], axis=1
            )
        )
    for g in range(parts):
        out_ref[g] = jnp.concatenate([row[g * side : (g + 1) * side] for row in rows], axis=0)


def products(op_blocks, near, own, cols, slots, parts):
    count_rows, terms, part_rows, _ = op_blocks.shape
    side = M // parts
    return pl.pallas_call(
        functools.partial(product_kernel, terms, parts),
        out_shape=jax.ShapeDtypeStruct((parts, count_rows * side, KC * M), F32),
        grid_spec=pltpu.PrefetchScalarGridSpec(
            num_scalar_prefetch=2,
            grid=(count_rows // QUAD,),
            in_specs=[
                pl.BlockSpec((QUAD, terms, part_rows, B), lambda i, *_: (i, 0, 0, 0)),
                pl.BlockSpec(memory_space=pltpu.VMEM),
                pl.BlockSpec((QUAD, M, part_rows), lambda i, *_: (i, 0, 0)),
            ],
            out_specs=pl.BlockSpec((parts, QUAD * side, KC * M), lambda i, *_: (0, i, 0)),
            scratch_shapes=[pltpu.VMEM((QUAD, KC // 2, M, 2 * HALF), F32)],
        ),
        compiler_params=pltpu.CompilerParams(vmem_limit_bytes=48 << 20),
    )(cols, slots, op_blocks, near, own)


def exchange_kernel(
    count, parts, part_ref, src_ref, lab_ref, out_ref,
    rx1, tx2, rx2, pk, rxw, rxl, summed, ns, nr, ws, wr, ls, lr,
):
    wide = lax.axis_index("wide")
    me = lax.axis_index("narrow")
    near = me + 1 - 2 * (me % 2)
    far = (me + 2) % parts
    cross = (near + 2) % parts
    barrier = pltpu.get_barrier_semaphore()
    pl.semaphore_signal(barrier, inc=1, device_id=(wide, near), device_id_type=MESH)
    pl.semaphore_signal(barrier, inc=1, device_id=(wide, far), device_id_type=MESH)

    @pl.loop(1, count)
    def _(d):
        pl.semaphore_signal(barrier, inc=1, device_id=((wide + d) % count, me), device_id_type=MESH)

    pl.semaphore_wait(barrier, count + 1)

    def remote(src, dst, s, r, target):
        return pltpu.make_async_remote_copy(
            src_ref=src, dst_ref=dst, send_sem=s, recv_sem=r, device_id=target, device_id_type=MESH
        )

    first = remote(part_ref.at[cross], rx1.at[1], ns.at[1], nr.at[1], (wide, near))
    second = remote(part_ref.at[near], rx1.at[0], ns.at[0], nr.at[0], (wide, near))
    third = remote(tx2, rx2, ns.at[2], nr.at[2], (wide, far))
    first.start()
    second.start()
    first.wait()
    tx2[...] = (part_ref[far] + rx1[1]).astype(BF16)
    third.start()
    second.wait()
    third.wait()
    summed[...] = (part_ref[me] + rx1[0] + rx2[...].astype(F32)).astype(BF16)

    height = pk.shape[1]
    lanes = lax.broadcasted_iota(I32, (height, summed.shape[0]), 1)

    def send(d):
        other = (wide + d) % count
        return (
            remote(pk.at[d], rxw.at[d], ws.at[d], wr.at[d], (other, me)),
            remote(lab_ref.at[other], rxl.at[d], ls.at[d], lr.at[d], (other, me)),
        )

    def packed(d):
        pick = (src_ref[(wide + d) % count] == lanes).astype(F32).astype(BF16)
        pk[d] = jnp.dot(pick, summed[...], preferred_element_type=F32).astype(BF16)

    @pl.loop(1, count)
    def _(d):
        packed(d)
        for copy in send(d):
            copy.start()

    packed(0)
    places = lax.broadcasted_iota(I32, (out_ref.shape[0], height), 0)

    def placed(labels, rows):
        pick = (labels == places).astype(F32).astype(BF16)
        return jnp.dot(pick, rows, preferred_element_type=F32)

    out_ref[...] = placed(lab_ref[wide], pk[0])

    @pl.loop(1, count)
    def _(d):
        for copy in send(d):
            copy.wait()
        out_ref[...] += placed(rxl[d], rxw[d])


def exchange(part, src, lab, parts, side):
    rows, columns = part.shape[1:]
    count, _, height = lab.shape
    vmem = pl.BlockSpec(memory_space=pltpu.VMEM)
    dma = pltpu.SemaphoreType.DMA
    return pl.pallas_call(
        functools.partial(exchange_kernel, count, parts),
        out_shape=jax.ShapeDtypeStruct((AGG_DEV * side, columns), F32),
        in_specs=[vmem] * 3,
        out_specs=vmem,
        scratch_shapes=[
            pltpu.VMEM((2, rows, columns), F32),
            pltpu.VMEM((rows, columns), BF16),
            pltpu.VMEM((rows, columns), BF16),
            pltpu.VMEM((count, height, columns), BF16),
            pltpu.VMEM((count, height, columns), BF16),
            pltpu.VMEM((count, 1, height), I32),
            pltpu.VMEM((rows, columns), BF16),
            dma((3,)), dma((3,)), dma((count,)), dma((count,)), dma((count,)), dma((count,)),
        ],
        compiler_params=pltpu.CompilerParams(
            collective_id=0, has_side_effects=True, vmem_limit_bytes=48 << 20
        ),
    )(part, src, lab)


def routes(owner, local, count, capacity, side):
    rows = owner.shape[0]
    index = jnp.arange(rows, dtype=I32)
    earlier = (owner[:, None] == owner[None, :]) & (index[None, :] < index[:, None])
    rank = jnp.sum(earlier.astype(I32), axis=1)
    height = -(-capacity * side // 16) * 16
    place = jnp.arange(height, dtype=I32)
    wanted = jnp.arange(count, dtype=I32)[:, None] * capacity + place[None, :] // side
    wanted = jnp.where(place[None, :] < capacity * side, wanted, -1)
    match = wanted[:, :, None] == (owner * capacity + rank)[None, None, :]
    filled = jnp.any(match, axis=2)
    inner = place[None, :] % side

    def spread(values):
        picked = jnp.sum(jnp.where(match, values[None, None, :], 0), axis=2)
        return jnp.where(filled, picked * side + inner, -1)

    return spread(index)[:, :, None], spread(local)[:, None, :]


def on_device(op_blocks, prolong, col_index, slot_index, dest_owner, dest_local):
    count_rows, _, part_rows, _ = op_blocks.shape
    count = lax.axis_size("wide")
    parts = lax.axis_size("narrow")
    wide_pos = lax.axis_index("wide")
    capacity = max(2, 2 * count_rows // count)
    side = M // parts
    src, lab = routes(dest_owner[:, 0], dest_local, count, capacity, side)
    complete = lax.all_gather(prolong, "narrow", axis=1, tiled=True)
    nearby = padded(complete, "wide").reshape(3 * count_rows, B, M)
    gap = jnp.zeros((3 * count_rows, B, HALF - M), BF16)
    near = jnp.concatenate([nearby, gap, nearby, gap], axis=2)
    cols = col_index - wide_pos * count_rows + count_rows
    own = prolong.reshape(count_rows, part_rows, M).swapaxes(1, 2)
    part = products(op_blocks, near, own, cols.reshape(-1), slot_index.reshape(-1), parts)
    coarse = exchange(part, src, lab, parts, side)
    return coarse.reshape(AGG_DEV, side, KC * M)


def solution(mesh):
    in_specs = (
        P("wide", None, "narrow", None),
        P("wide", "narrow"),
        P("wide", None),
        P("wide", None),
        P("wide", None),
        P("wide"),
    )
    out_specs = P("wide", "narrow", None)
    return jax.shard_map(
        on_device, mesh=mesh, in_specs=in_specs, out_specs=out_specs, check_vma=False
    )
```

```python
import functools

import jax
import jax.numpy as jnp
from jax import lax
from jax.experimental import pallas as pl
from jax.experimental.pallas import tpu as pltpu
from jax.sharding import PartitionSpec as P

B = 192
M = 48
KC = 8
AGG_DEV = 16
HALF = 64
QUAD = 4
MESH = pl.DeviceIdType.MESH
F32 = jnp.float32
BF16 = jnp.bfloat16
I32 = jnp.int32


def gather_kernel(count, parts, chunks, own_ref, near_ref, ss, rs, keep_sem):
    wide = lax.axis_index("wide")
    me = lax.axis_index("narrow")
    near = me + 1 - 2 * (me % 2)
    far = (me + 2) % parts
    pairs, depth, _ = own_ref.shape
    piece = pairs // chunks
    first, last = wide == 0, wide == count - 1
    has = {0: jnp.logical_not(first), 1: None, 2: jnp.logical_not(last)}
    barrier = pltpu.get_barrier_semaphore()

    def when(cond, fn):
        fn() if cond is None else pl.when(cond)(fn)

    def hello(where):
        pl.semaphore_signal(barrier, inc=1, device_id=where, device_id_type=MESH)

    hello((wide, near))
    hello((wide, far))
    when(has[0], lambda: hello((wide - 1, me)))
    when(has[2], lambda: hello((wide + 1, me)))
    sides = (wide + count - 1) // count + (2 * count - 2 - wide) // count
    pl.semaphore_wait(barrier, 2 + sides)

    def place(slot, part, c):
        return near_ref.at[pl.ds(slot * pairs + c * piece, piece), pl.ds(part * depth, depth)]

    def remote(slot, kind, c, target, source, part):
        return pltpu.make_async_remote_copy(
            src_ref=source,
            dst_ref=place(slot, part, c),
            send_sem=ss.at[slot, kind, c],
            recv_sem=rs.at[slot, kind, c],
            device_id=target,
            device_id_type=MESH,
        )

    def mine(c):
        return own_ref.at[pl.ds(c * piece, piece)]

    def direct(slot, c):
        target = (wide + 1 if slot == 0 else wide - 1, me)
        return remote(slot, 0, c, target, mine(c), me)

    def held(slot, c):
        return mine(c) if slot == 1 else place(slot, me, c)

    def to_near(slot, c):
        return remote(slot, 1, c, (wide, near), held(slot, c), me)

    def to_far(slot, c):
        return remote(slot, 2, c, (wide, far), held(slot, c), me)

    def onward(slot, c):
        return remote(slot, 3, c, (wide, near), place(slot, far, c), far)

    keep = pltpu.make_async_copy(
        own_ref, near_ref.at[pl.ds(pairs, pairs), pl.ds(me * depth, depth)], keep_sem
    )
    for c in range(chunks):
        to_far(1, c).start()
        when(has[2], lambda: direct(0, c).start())
        when(has[0], lambda: direct(2, c).start())
        to_near(1, c).start()
    keep.start()

    def spread(slot, c):
        direct(slot, c).wait_recv()
        to_far(slot, c).start()
        to_near(slot, c).start()

    def forward(slot, c):
        to_far(slot, c).wait_recv()
        onward(slot, c).start()

    for c in range(chunks):
        forward(1, c)
        when(has[0], lambda: spread(0, c))
        when(has[2], lambda: spread(2, c))
    for c in range(chunks):
        when(has[0], lambda: forward(0, c))
        when(has[2], lambda: forward(2, c))

    def drain(slot):
        for c in range(chunks):
            to_near(slot, c).wait()
            to_far(slot, c).wait_send()
            onward(slot, c).wait()

    for slot in range(3):
        when(has[slot], lambda: drain(slot))
    for c in range(chunks):
        when(has[2], lambda: direct(0, c).wait_send())
        when(has[0], lambda: direct(2, c).wait_send())
    keep.wait()


def gathered(own, count, parts, chunks=4):
    pairs, depth, lanes = own.shape
    hbm = pl.BlockSpec(memory_space=pl.ANY)
    sems = pltpu.SemaphoreType.DMA((3, 4, chunks))
    return pl.pallas_call(
        functools.partial(gather_kernel, count, parts, chunks),
        out_shape=jax.ShapeDtypeStruct((3 * pairs, parts * depth, lanes), BF16),
        in_specs=[hbm],
        out_specs=hbm,
        scratch_shapes=[sems, sems, pltpu.SemaphoreType.DMA],
        compiler_params=pltpu.CompilerParams(collective_id=1, has_side_effects=True),
    )(own)


def product_kernel(terms, parts, tile_ref, swap_ref, slot_ref, op_ref, near_ref, own_ref, out_ref, acc):
    step = pl.program_id(0)
    side = M // parts
    lane_half = lax.broadcasted_iota(I32, (M, 2 * HALF), 1) // HALF
    rows = []
    for j in range(QUAD):
        base = (step * QUAD + j) * terms
        acc[j] = jnp.zeros_like(acc[j])
        applied = [
            jnp.dot(op_ref[j, k], near_ref[tile_ref[base + k]], preferred_element_type=F32).astype(BF16)
            for k in range(terms)
        ]
        projected = jnp.dot(own_ref[j], jnp.concatenate(applied, axis=1), preferred_element_type=F32)
        for k in range(terms):
            slot = slot_ref[base + k]
            piece = projected[:, k * 2 * HALF : (k + 1) * 2 * HALF]
            piece = jnp.where(swap_ref[base + k] == 1, pltpu.roll(piece, HALF, 1), piece)
            acc[j, slot // 2] += jnp.where(lane_half == slot % 2, piece, 0.0)
        rows.append(
            jnp.concatenate(
                [acc[j, s // 2][:, (s % 2) * HALF : (s % 2) * HALF + M] for s in range(KC)], axis=1
            )
        )
    for g in range(parts):
        out_ref[g] = jnp.concatenate([row[g * side : (g + 1) * side] for row in rows], axis=0)


def products(op_blocks, near, own, tiles, swaps, slots, parts):
    count_rows, terms, part_rows, _ = op_blocks.shape
    side = M // parts
    return pl.pallas_call(
        functools.partial(product_kernel, terms, parts),
        out_shape=jax.ShapeDtypeStruct((parts, count_rows * side, KC * M), F32),
        grid_spec=pltpu.PrefetchScalarGridSpec(
            num_scalar_prefetch=3,
            grid=(count_rows // QUAD,),
            in_specs=[
                pl.BlockSpec((QUAD, terms, part_rows, B), lambda i, *_: (i, 0, 0, 0)),
                pl.BlockSpec(memory_space=pltpu.VMEM),
                pl.BlockSpec((QUAD, M, part_rows), lambda i, *_: (i, 0, 0)),
            ],
            out_specs=pl.BlockSpec((parts, QUAD * side, KC * M), lambda i, *_: (0, i, 0)),
            scratch_shapes=[pltpu.VMEM((QUAD, KC // 2, M, 2 * HALF), F32)],
        ),
        compiler_params=pltpu.CompilerParams(vmem_limit_bytes=48 << 20),
    )(tiles, swaps, slots, op_blocks, near, own)


def exchange_kernel(
    count, parts, part_ref, src_ref, lab_ref, out_ref,
    rx1, tx2, rx2, pk, rxw, rxl, summed, ns, nr, ws, wr, ls, lr,
):
    wide = lax.axis_index("wide")
    me = lax.axis_index("narrow")
    near = me + 1 - 2 * (me % 2)
    far = (me + 2) % parts
    cross = (near + 2) % parts
    barrier = pltpu.get_barrier_semaphore()
    pl.semaphore_signal(barrier, inc=1, device_id=(wide, near), device_id_type=MESH)
    pl.semaphore_signal(barrier, inc=1, device_id=(wide, far), device_id_type=MESH)

    @pl.loop(1, count)
    def _(d):
        pl.semaphore_signal(barrier, inc=1, device_id=((wide + d) % count, me), device_id_type=MESH)

    pl.semaphore_wait(barrier, count + 1)

    def remote(src, dst, s, r, target):
        return pltpu.make_async_remote_copy(
            src_ref=src, dst_ref=dst, send_sem=s, recv_sem=r, device_id=target, device_id_type=MESH
        )

    first = remote(part_ref.at[cross], rx1.at[1], ns.at[1], nr.at[1], (wide, near))
    second = remote(part_ref.at[near], rx1.at[0], ns.at[0], nr.at[0], (wide, near))
    third = remote(tx2, rx2, ns.at[2], nr.at[2], (wide, far))
    first.start()
    second.start()
    first.wait()
    tx2[...] = (part_ref[far] + rx1[1]).astype(BF16)
    third.start()
    second.wait()
    third.wait()
    summed[...] = (part_ref[me] + rx1[0] + rx2[...].astype(F32)).astype(BF16)

    height = pk.shape[1]
    lanes = lax.broadcasted_iota(I32, (height, summed.shape[0]), 1)

    def send(d):
        other = (wide + d) % count
        return (
            remote(pk.at[d], rxw.at[d], ws.at[d], wr.at[d], (other, me)),
            remote(lab_ref.at[other], rxl.at[d], ls.at[d], lr.at[d], (other, me)),
        )

    def packed(d):
        pick = (src_ref[(wide + d) % count] == lanes).astype(F32).astype(BF16)
        pk[d] = jnp.dot(pick, summed[...], preferred_element_type=F32).astype(BF16)

    @pl.loop(1, count)
    def _(d):
        packed(d)
        for copy in send(d):
            copy.start()

    packed(0)
    places = lax.broadcasted_iota(I32, (out_ref.shape[0], height), 0)

    def placed(labels, rows):
        pick = (labels == places).astype(F32).astype(BF16)
        return jnp.dot(pick, rows, preferred_element_type=F32)

    out_ref[...] = placed(lab_ref[wide], pk[0])

    @pl.loop(1, count)
    def _(d):
        for copy in send(d):
            copy.wait()
        out_ref[...] += placed(rxl[d], rxw[d])


def exchange(part, src, lab, parts, side):
    rows, columns = part.shape[1:]
    count, _, height = lab.shape
    vmem = pl.BlockSpec(memory_space=pltpu.VMEM)
    dma = pltpu.SemaphoreType.DMA
    return pl.pallas_call(
        functools.partial(exchange_kernel, count, parts),
        out_shape=jax.ShapeDtypeStruct((AGG_DEV * side, columns), F32),
        in_specs=[vmem] * 3,
        out_specs=vmem,
        scratch_shapes=[
            pltpu.VMEM((2, rows, columns), F32),
            pltpu.VMEM((rows, columns), BF16),
            pltpu.VMEM((rows, columns), BF16),
            pltpu.VMEM((count, height, columns), BF16),
            pltpu.VMEM((count, height, columns), BF16),
            pltpu.VMEM((count, 1, height), I32),
            pltpu.VMEM((rows, columns), BF16),
            dma((3,)), dma((3,)), dma((count,)), dma((count,)), dma((count,)), dma((count,)),
        ],
        compiler_params=pltpu.CompilerParams(
            collective_id=0, has_side_effects=True, vmem_limit_bytes=48 << 20
        ),
    )(part, src, lab)


def routes(owner, local, count, capacity, side):
    rows = owner.shape[0]
    index = jnp.arange(rows, dtype=I32)
    earlier = (owner[:, None] == owner[None, :]) & (index[None, :] < index[:, None])
    rank = jnp.sum(earlier.astype(I32), axis=1)
    height = -(-capacity * side // 16) * 16
    place = jnp.arange(height, dtype=I32)
    wanted = jnp.arange(count, dtype=I32)[:, None] * capacity + place[None, :] // side
    wanted = jnp.where(place[None, :] < capacity * side, wanted, -1)
    match = wanted[:, :, None] == (owner * capacity + rank)[None, None, :]
    filled = jnp.any(match, axis=2)
    inner = place[None, :] % side

    def spread(values):
        picked = jnp.sum(jnp.where(match, values[None, None, :], 0), axis=2)
        return jnp.where(filled, picked * side + inner, -1)

    return spread(index)[:, :, None], spread(local)[:, None, :]


def on_device(op_blocks, prolong, col_index, slot_index, dest_owner, dest_local):
    count_rows, _, part_rows, _ = op_blocks.shape
    count = lax.axis_size("wide")
    parts = lax.axis_size("narrow")
    wide_pos = lax.axis_index("wide")
    capacity = max(2, 2 * count_rows // count)
    side = M // parts
    src, lab = routes(dest_owner[:, 0], dest_local, count, capacity, side)
    pairs = count_rows // 2
    blocks = prolong.reshape(count_rows, part_rows, M)
    gap = jnp.zeros((pairs, part_rows, HALF - M), BF16)
    paired = jnp.concatenate([blocks[:pairs], gap, blocks[pairs:], gap], axis=2)
    near = gathered(paired, count, parts)
    cols = (col_index - wide_pos * count_rows + count_rows).reshape(-1)
    slots = slot_index.reshape(-1)
    inner = cols % count_rows
    tiles = cols // count_rows * pairs + inner % pairs
    swaps = (inner // pairs + slots) % 2
    part = products(op_blocks, near, blocks.swapaxes(1, 2), tiles, swaps, slots, parts)
    coarse = exchange(part, src, lab, parts, side)
    return coarse.reshape(AGG_DEV, side, KC * M)


def solution(mesh):
    in_specs = (
        P("wide", None, "narrow", None),
        P("wide", "narrow"),
        P("wide", None),
        P("wide", None),
        P("wide", None),
        P("wide"),
    )
    out_specs = P("wide", "narrow", None)
    return jax.shard_map(
        on_device, mesh=mesh, in_specs=in_specs, out_specs=out_specs, check_vma=False
    )
```

```python
import functools

import jax
import jax.numpy as jnp
from jax import lax
from jax.experimental import pallas as pl
from jax.experimental.pallas import tpu as pltpu
from jax.sharding import PartitionSpec as P

B = 192
M = 48
KC = 8
AGG_DEV = 16
HALF = 64
QUAD = 4
MESH = pl.DeviceIdType.MESH
F32 = jnp.float32
BF16 = jnp.bfloat16
I32 = jnp.int32


def gather_kernel(count, parts, chunks, own_ref, near_ref, ss, rs, keep_sem):
    wide = lax.axis_index("wide")
    me = lax.axis_index("narrow")
    near = me + 1 - 2 * (me % 2)
    far = (me + 2) % parts
    pairs, depth, _ = own_ref.shape
    piece = pairs // chunks
    first, last = wide == 0, wide == count - 1
    has = {0: jnp.logical_not(first), 1: None, 2: jnp.logical_not(last)}
    barrier = pltpu.get_barrier_semaphore()

    def when(cond, fn):
        fn() if cond is None else pl.when(cond)(fn)

    def hello(where):
        pl.semaphore_signal(barrier, inc=1, device_id=where, device_id_type=MESH)

    hello((wide, near))
    hello((wide, far))
    when(has[0], lambda: hello((wide - 1, me)))
    when(has[2], lambda: hello((wide + 1, me)))
    sides = (wide + count - 1) // count + (2 * count - 2 - wide) // count
    pl.semaphore_wait(barrier, 2 + sides)

    def place(slot, part, c):
        return near_ref.at[pl.ds(slot * pairs + c * piece, piece), pl.ds(part * depth, depth)]

    def remote(slot, kind, c, target, source, part):
        return pltpu.make_async_remote_copy(
            src_ref=source,
            dst_ref=place(slot, part, c),
            send_sem=ss.at[slot, kind, c],
            recv_sem=rs.at[slot, kind, c],
            device_id=target,
            device_id_type=MESH,
        )

    def mine(c):
        return own_ref.at[pl.ds(c * piece, piece)]

    def direct(slot, c):
        target = (wide + 1 if slot == 0 else wide - 1, me)
        return remote(slot, 0, c, target, mine(c), me)

    def held(slot, c):
        return mine(c) if slot == 1 else place(slot, me, c)

    def to_near(slot, c):
        return remote(slot, 1, c, (wide, near), held(slot, c), me)

    def to_far(slot, c):
        return remote(slot, 2, c, (wide, far), held(slot, c), me)

    def onward(slot, c):
        return remote(slot, 3, c, (wide, near), place(slot, far, c), far)

    keep = pltpu.make_async_copy(
        own_ref, near_ref.at[pl.ds(pairs, pairs), pl.ds(me * depth, depth)], keep_sem
    )
    for c in range(chunks):
        to_far(1, c).start()
        when(has[2], lambda: direct(0, c).start())
        when(has[0], lambda: direct(2, c).start())
        to_near(1, c).start()
    keep.start()

    def spread(slot, c):
        direct(slot, c).wait_recv()
        to_far(slot, c).start()
        to_near(slot, c).start()

    def forward(slot, c):
        to_far(slot, c).wait_recv()
        onward(slot, c).start()

    for c in range(chunks):
        forward(1, c)
        when(has[0], lambda: spread(0, c))
        when(has[2], lambda: spread(2, c))
    for c in range(chunks):
        when(has[0], lambda: forward(0, c))
        when(has[2], lambda: forward(2, c))

    def drain(slot):
        for c in range(chunks):
            to_near(slot, c).wait()
            to_far(slot, c).wait_send()
            onward(slot, c).wait()

    for slot in range(3):
        when(has[slot], lambda: drain(slot))
    for c in range(chunks):
        when(has[2], lambda: direct(0, c).wait_send())
        when(has[0], lambda: direct(2, c).wait_send())
    keep.wait()


def gathered(own, count, parts, chunks=4):
    pairs, depth, lanes = own.shape
    hbm = pl.BlockSpec(memory_space=pl.ANY)
    sems = pltpu.SemaphoreType.DMA((3, 4, chunks))
    return pl.pallas_call(
        functools.partial(gather_kernel, count, parts, chunks),
        out_shape=jax.ShapeDtypeStruct((3 * pairs, parts * depth, lanes), BF16),
        in_specs=[hbm],
        out_specs=hbm,
        scratch_shapes=[sems, sems, pltpu.SemaphoreType.DMA],
        compiler_params=pltpu.CompilerParams(collective_id=1, has_side_effects=True),
    )(own)


def coarse_kernel(
    count, parts, terms, steps, chunks,
    tile_ref, swap_ref, slot_ref, op_ref, near_ref, own_ref, src_ref, lab_ref, out_ref,
    part, rx1, tx2, rx2, pk, rxw, rxl, summed, ns, nr, ws, wr, ls, lr,
):
    step = pl.program_id(0)
    wide = lax.axis_index("wide")
    me = lax.axis_index("narrow")
    near = me + 1 - 2 * (me % 2)
    far = (me + 2) % parts
    cross = (near + 2) % parts
    side = M // parts
    per = steps // chunks
    height = pk.shape[1]
    chunk_rows = summed.shape[0] // chunks

    def remote(src, dst, s, r, target):
        return pltpu.make_async_remote_copy(
            src_ref=src, dst_ref=dst, send_sem=s, recv_sem=r, device_id=target, device_id_type=MESH
        )

    def rows_of(q):
        return pl.ds(pl.multiple_of(q * chunk_rows, chunk_rows), chunk_rows)

    def first(q):
        r = rows_of(q)
        return remote(part.at[cross, r], rx1.at[1, r], ns.at[0, q], nr.at[0, q], (wide, near))

    def second(q):
        r = rows_of(q)
        return remote(part.at[near, r], rx1.at[0, r], ns.at[1, q], nr.at[1, q], (wide, near))

    def third(q):
        r = rows_of(q)
        return remote(tx2.at[r], rx2.at[r], ns.at[2, q], nr.at[2, q], (wide, far))

    def relay(q):
        r = rows_of(q)
        first(q).wait()
        tx2[r] = (part[far, r] + rx1[1, r]).astype(BF16)
        third(q).start()

    def finish(q):
        r = rows_of(q)
        second(q).wait()
        third(q).wait()
        summed[r] = (part[me, r] + rx1[0, r] + rx2[r].astype(F32)).astype(BF16)

    def send(d):
        other = (wide + d) % count
        return (
            remote(pk.at[d], rxw.at[d], ws.at[d], wr.at[d], (other, me)),
            remote(lab_ref.at[other], rxl.at[d], ls.at[d], lr.at[d], (other, me)),
        )

    def packed(d):
        lanes = lax.broadcasted_iota(I32, (height, summed.shape[0]), 1)
        pick = (src_ref[(wide + d) % count] == lanes).astype(F32).astype(BF16)
        pk[d] = jnp.dot(pick, summed[...], preferred_element_type=F32).astype(BF16)

    def placed(labels, rows):
        places = lax.broadcasted_iota(I32, (out_ref.shape[0], height), 0)
        pick = (labels == places).astype(F32).astype(BF16)
        return jnp.dot(pick, rows, preferred_element_type=F32)

    @pl.when(step == 0)
    def _():
        barrier = pltpu.get_barrier_semaphore()
        pl.semaphore_signal(barrier, inc=1, device_id=(wide, near), device_id_type=MESH)
        pl.semaphore_signal(barrier, inc=1, device_id=(wide, far), device_id_type=MESH)

        @pl.loop(1, count)
        def _(d):
            pl.semaphore_signal(
                barrier, inc=1, device_id=((wide + d) % count, me), device_id_type=MESH
            )

        pl.semaphore_wait(barrier, count + 1)

    lane_half = lax.broadcasted_iota(I32, (1, 2 * HALF), 1) // HALF
    rows = []
    for j in range(QUAD):
        base = (step * QUAD + j) * terms
        applied = [
            jnp.dot(op_ref[j, k], near_ref[tile_ref[base + k]], preferred_element_type=F32).astype(BF16)
            for k in range(terms)
        ]
        projected = jnp.dot(own_ref[j], jnp.concatenate(applied, axis=1), preferred_element_type=F32)
        sums = [jnp.zeros((M, 2 * HALF), F32) for _ in range(KC // 2)]
        for k in range(terms):
            slot = slot_ref[base + k]
            piece = projected[:, k * 2 * HALF : (k + 1) * 2 * HALF]
            piece = jnp.where(swap_ref[base + k] == 1, pltpu.roll(piece, HALF, 1), piece)
            for t in range(KC // 2):
                sums[t] = sums[t] + jnp.where(lane_half + 2 * t == slot, piece, 0.0)
        rows.append(
            jnp.concatenate(
                [sums[s // 2][:, (s % 2) * HALF : (s % 2) * HALF + M] for s in range(KC)], axis=1
            )
        )
    at = pl.ds(pl.multiple_of(step * (QUAD * side), QUAD * side), QUAD * side)
    for g in range(parts):
        part[g, at] = jnp.concatenate([row[g * side : (g + 1) * side] for row in rows], axis=0)

    @pl.when(step % per == per - 1)
    def _():
        first(step // per).start()
        second(step // per).start()

    @pl.when((step % per == per // 2) & (step >= per))
    def _():
        relay(step // per - 1)

    @pl.when(step == steps - 1)
    def _():
        relay(chunks - 1)
        for q in range(chunks):
            finish(q)

        @pl.loop(1, count)
        def _(d):
            packed(d)
            for copy in send(d):
                copy.start()

        packed(0)
        out_ref[...] = placed(lab_ref[wide], pk[0])

        @pl.loop(1, count)
        def _(d):
            for copy in send(d):
                copy.wait()
            out_ref[...] += placed(rxl[d], rxw[d])


def coarse_rows(op_blocks, near, own, tiles, swaps, slots, src, lab, parts, chunks=4):
    count_rows, terms, part_rows, _ = op_blocks.shape
    side = M // parts
    count, _, height = lab.shape
    steps = count_rows // QUAD
    rows, columns = count_rows * side, KC * M
    vmem = pl.BlockSpec(memory_space=pltpu.VMEM)
    dma = pltpu.SemaphoreType.DMA
    return pl.pallas_call(
        functools.partial(coarse_kernel, count, parts, terms, steps, chunks),
        out_shape=jax.ShapeDtypeStruct((AGG_DEV * side, columns), F32),
        grid_spec=pltpu.PrefetchScalarGridSpec(
            num_scalar_prefetch=3,
            grid=(steps,),
            in_specs=[
                pl.BlockSpec((QUAD, terms, part_rows, B), lambda i, *_: (i, 0, 0, 0)),
                vmem,
                pl.BlockSpec((QUAD, M, part_rows), lambda i, *_: (i, 0, 0)),
                vmem,
                vmem,
            ],
            out_specs=pl.BlockSpec((AGG_DEV * side, columns), lambda i, *_: (0, 0)),
            scratch_shapes=[
                pltpu.VMEM((parts, rows, columns), F32),
                pltpu.VMEM((2, rows, columns), F32),
                pltpu.VMEM((rows, columns), BF16),
                pltpu.VMEM((rows, columns), BF16),
                pltpu.VMEM((count, height, columns), BF16),
                pltpu.VMEM((count, height, columns), BF16),
                pltpu.VMEM((count, 1, height), I32),
                pltpu.VMEM((rows, columns), BF16),
                dma((3, chunks)), dma((3, chunks)),
                dma((count,)), dma((count,)), dma((count,)), dma((count,)),
            ],
        ),
        compiler_params=pltpu.CompilerParams(
            collective_id=0, has_side_effects=True, vmem_limit_bytes=48 << 20
        ),
    )(tiles, swaps, slots, op_blocks, near, own, src, lab)


def routes(owner, local, count, capacity, side):
    rows = owner.shape[0]
    index = jnp.arange(rows, dtype=I32)
    earlier = (owner[:, None] == owner[None, :]) & (index[None, :] < index[:, None])
    rank = jnp.sum(earlier.astype(I32), axis=1)
    height = -(-capacity * side // 16) * 16
    place = jnp.arange(height, dtype=I32)
    wanted = jnp.arange(count, dtype=I32)[:, None] * capacity + place[None, :] // side
    wanted = jnp.where(place[None, :] < capacity * side, wanted, -1)
    match = wanted[:, :, None] == (owner * capacity + rank)[None, None, :]
    filled = jnp.any(match, axis=2)
    inner = place[None, :] % side

    def spread(values):
        picked = jnp.sum(jnp.where(match, values[None, None, :], 0), axis=2)
        return jnp.where(filled, picked * side + inner, -1)

    return spread(index)[:, :, None], spread(local)[:, None, :]


def on_device(op_blocks, prolong, col_index, slot_index, dest_owner, dest_local):
    count_rows, _, part_rows, _ = op_blocks.shape
    count = lax.axis_size("wide")
    parts = lax.axis_size("narrow")
    wide_pos = lax.axis_index("wide")
    capacity = max(2, 2 * count_rows // count)
    side = M // parts
    src, lab = routes(dest_owner[:, 0], dest_local, count, capacity, side)
    pairs = count_rows // 2
    blocks = prolong.reshape(count_rows, part_rows, M)
    gap = jnp.zeros((pairs, part_rows, HALF - M), BF16)
    paired = jnp.concatenate([blocks[:pairs], gap, blocks[pairs:], gap], axis=2)
    near = gathered(paired, count, parts)
    cols = (col_index - wide_pos * count_rows + count_rows).reshape(-1)
    slots = slot_index.reshape(-1)
    inner = cols % count_rows
    tiles = cols // count_rows * pairs + inner % pairs
    swaps = (inner // pairs + slots) % 2
    coarse = coarse_rows(
        op_blocks, near, blocks.swapaxes(1, 2), tiles, swaps, slots, src, lab, parts
    )
    return coarse.reshape(AGG_DEV, side, KC * M)


def solution(mesh):
    in_specs = (
        P("wide", None, "narrow", None),
        P("wide", "narrow"),
        P("wide", None),
        P("wide", None),
        P("wide", None),
        P("wide"),
    )
    out_specs = P("wide", "narrow", None)
    return jax.shard_map(
        on_device, mesh=mesh, in_specs=in_specs, out_specs=out_specs, check_vma=False
    )
```

```python
import functools

import jax
import jax.numpy as jnp
from jax import lax
from jax.experimental import pallas as pl
from jax.experimental.pallas import tpu as pltpu
from jax.sharding import PartitionSpec as P

B = 192
M = 48
KC = 8
AGG_DEV = 16
HALF = 64
QUAD = 4
ROWS = 8
MESH = pl.DeviceIdType.MESH
F32 = jnp.float32
BF16 = jnp.bfloat16
I32 = jnp.int32


def gather_kernel(count, parts, chunks, own_ref, near_ref, ss, rs, keep_sem):
    wide = lax.axis_index("wide")
    me = lax.axis_index("narrow")
    near = me + 1 - 2 * (me % 2)
    far = (me + 2) % parts
    pairs, depth, _ = own_ref.shape
    piece = pairs // chunks
    first, last = wide == 0, wide == count - 1
    has = {0: jnp.logical_not(first), 1: None, 2: jnp.logical_not(last)}
    barrier = pltpu.get_barrier_semaphore()

    def when(cond, fn):
        fn() if cond is None else pl.when(cond)(fn)

    def hello(where):
        pl.semaphore_signal(barrier, inc=1, device_id=where, device_id_type=MESH)

    hello((wide, near))
    hello((wide, far))
    when(has[0], lambda: hello((wide - 1, me)))
    when(has[2], lambda: hello((wide + 1, me)))
    sides = (wide + count - 1) // count + (2 * count - 2 - wide) // count
    pl.semaphore_wait(barrier, 2 + sides)

    def place(slot, part, c):
        return near_ref.at[pl.ds(slot * pairs + c * piece, piece), pl.ds(part * depth, depth)]

    def remote(slot, kind, c, target, source, part, sent=None):
        return pltpu.make_async_remote_copy(
            src_ref=source,
            dst_ref=place(slot, part, c),
            send_sem=ss.at[slot, kind if sent is None else sent, c],
            recv_sem=rs.at[slot, kind, c],
            device_id=target,
            device_id_type=MESH,
        )

    def mine(c):
        return own_ref.at[pl.ds(c * piece, piece)]

    def direct(slot, c):
        target = (wide + 1 if slot == 0 else wide - 1, me)
        return remote(slot, 0, c, target, mine(c), me)

    def held(slot, c):
        return mine(c) if slot == 1 else place(slot, me, c)

    def to_near(slot, c):
        return remote(slot, 1, c, (wide, near), held(slot, c), me)

    def to_far(slot, c):
        return remote(slot, 2, c, (wide, far), held(slot, c), me)

    def onward(slot, c):
        return remote(slot, 3, c, (wide, near), place(slot, far, c), far)

    keep = pltpu.make_async_copy(
        own_ref, near_ref.at[pl.ds(pairs, pairs), pl.ds(me * depth, depth)], keep_sem
    )
    for c in range(chunks):
        to_far(1, c).start()
        when(has[2], lambda: direct(0, c).start())
        when(has[0], lambda: direct(2, c).start())
        to_near(1, c).start()
    keep.start()

    def across(slot, c):
        target = (wide + 1 if slot == 0 else wide - 1, me)
        return remote(slot, 2, c, target, place(1, far, c), far, sent=4)

    twin = {0: has[2] & (wide % 2 == 0), 2: wide % 2 == 1}
    paired = {0: wide % 2 == 1, 2: has[2] & (wide % 2 == 0)}
    detour = [c for c in range(chunks) if c < chunks // 2]

    def spread(slot, c):
        direct(slot, c).wait_recv()
        to_near(slot, c).start()
        if c in detour:
            pl.when(jnp.logical_not(paired[slot]))(lambda: to_far(slot, c).start())
        else:
            to_far(slot, c).start()

    def forward(slot, c):
        to_far(slot, c).wait_recv()
        onward(slot, c).start()
        if slot == 1 and c in detour:
            for there in (0, 2):
                pl.when(twin[there])(lambda: across(there, c).start())

    for c in range(chunks):
        forward(1, c)
        when(has[0], lambda: spread(0, c))
        when(has[2], lambda: spread(2, c))
    for c in range(chunks):
        when(has[0], lambda: forward(0, c))
        when(has[2], lambda: forward(2, c))

    def drain(slot):
        for c in range(chunks):
            to_near(slot, c).wait()
            if slot != 1 and c in detour:
                pl.when(jnp.logical_not(paired[slot]))(lambda: to_far(slot, c).wait_send())
            else:
                to_far(slot, c).wait_send()
            onward(slot, c).wait()

    for slot in range(3):
        when(has[slot], lambda: drain(slot))
    for c in detour:
        for there in (0, 2):
            pl.when(twin[there])(lambda: across(there, c).wait_send())
    for c in range(chunks):
        when(has[2], lambda: direct(0, c).wait_send())
        when(has[0], lambda: direct(2, c).wait_send())
    keep.wait()


def gathered(own, count, parts, chunks=4):
    pairs, depth, lanes = own.shape
    hbm = pl.BlockSpec(memory_space=pl.ANY)
    sems = pltpu.SemaphoreType.DMA((3, 5, chunks))
    return pl.pallas_call(
        functools.partial(gather_kernel, count, parts, chunks),
        out_shape=jax.ShapeDtypeStruct((3 * pairs, parts * depth, lanes), BF16),
        in_specs=[hbm],
        out_specs=hbm,
        scratch_shapes=[sems, sems, pltpu.SemaphoreType.DMA],
        compiler_params=pltpu.CompilerParams(collective_id=1, has_side_effects=True),
    )(own)


def coarse_kernel(
    count, parts, terms, steps, chunks,
    tile_ref, swap_ref, slot_ref, op_ref, near_ref, own_ref, src_ref, lab_ref, out_ref,
    part, rx1, tx2, rx2, pk, rxw, rxl, summed, ns, nr, ws, wr, ls, lr,
):
    step = pl.program_id(0)
    wide = lax.axis_index("wide")
    me = lax.axis_index("narrow")
    near = me + 1 - 2 * (me % 2)
    far = (me + 2) % parts
    cross = (near + 2) % parts
    side = M // parts
    per = steps // chunks
    height = pk.shape[1]
    chunk_rows = summed.shape[0] // chunks

    def remote(src, dst, s, r, target):
        return pltpu.make_async_remote_copy(
            src_ref=src, dst_ref=dst, send_sem=s, recv_sem=r, device_id=target, device_id_type=MESH
        )

    def rows_of(q):
        return pl.ds(pl.multiple_of(q * chunk_rows, chunk_rows), chunk_rows)

    def first(q):
        r = rows_of(q)
        return remote(part.at[cross, r], rx1.at[1, r], ns.at[0, q], nr.at[0, q], (wide, near))

    def second(q):
        r = rows_of(q)
        return remote(part.at[near, r], rx1.at[0, r], ns.at[1, q], nr.at[1, q], (wide, near))

    def third(q):
        r = rows_of(q)
        return remote(tx2.at[r], rx2.at[r], ns.at[2, q], nr.at[2, q], (wide, far))

    def relay(q):
        r = rows_of(q)
        first(q).wait()
        tx2[r] = (part[far, r] + rx1[1, r]).astype(BF16)
        third(q).start()

    def finish(q):
        r = rows_of(q)
        second(q).wait()
        third(q).wait()
        summed[r] = (part[me, r] + rx1[0, r] + rx2[r].astype(F32)).astype(BF16)

    def send(d):
        other = (wide + d) % count
        return (
            remote(pk.at[d], rxw.at[d], ws.at[d], wr.at[d], (other, me)),
            remote(lab_ref.at[other], rxl.at[d], ls.at[d], lr.at[d], (other, me)),
        )

    def packed(d):
        lanes = lax.broadcasted_iota(I32, (height, summed.shape[0]), 1)
        pick = (src_ref[(wide + d) % count] == lanes).astype(F32).astype(BF16)
        pk[d] = jnp.dot(pick, summed[...], preferred_element_type=F32).astype(BF16)

    def placed(labels, rows):
        places = lax.broadcasted_iota(I32, (out_ref.shape[0], height), 0)
        pick = (labels == places).astype(F32).astype(BF16)
        return jnp.dot(pick, rows, preferred_element_type=F32)

    @pl.when(step == 0)
    def _():
        barrier = pltpu.get_barrier_semaphore()
        pl.semaphore_signal(barrier, inc=1, device_id=(wide, near), device_id_type=MESH)
        pl.semaphore_signal(barrier, inc=1, device_id=(wide, far), device_id_type=MESH)

        @pl.loop(1, count)
        def _(d):
            pl.semaphore_signal(
                barrier, inc=1, device_id=((wide + d) % count, me), device_id_type=MESH
            )

        pl.semaphore_wait(barrier, count + 1)

    lane_half = lax.broadcasted_iota(I32, (1, 2 * HALF), 1) // HALF
    applied = []
    for j in range(ROWS):
        base = (step * ROWS + j) * terms
        for k in range(0, terms, 2):
            tiles = jnp.concatenate(
                [near_ref[tile_ref[base + k]], near_ref[tile_ref[base + k + 1]]], axis=1
            )
            stacked = op_ref[j, k : k + 2].reshape(-1, B)
            both = jnp.dot(stacked, tiles, preferred_element_type=F32)
            depth = both.shape[0] // 2
            applied.append(both[:depth, : 2 * HALF].astype(BF16))
            applied.append(both[depth:, 2 * HALF :].astype(BF16))
    rows = []
    for j in range(ROWS):
        base = (step * ROWS + j) * terms
        held = jnp.concatenate(applied[j * terms : (j + 1) * terms], axis=1)
        projected = jnp.dot(own_ref[j], held, preferred_element_type=F32)
        sums = [jnp.zeros((M, 2 * HALF), F32) for _ in range(KC // 2)]
        for k in range(terms):
            slot = slot_ref[base + k]
            piece = projected[:, k * 2 * HALF : (k + 1) * 2 * HALF]
            piece = jnp.where(swap_ref[base + k] == 1, pltpu.roll(piece, HALF, 1), piece)
            for t in range(KC // 2):
                sums[t] = sums[t] + jnp.where(lane_half + 2 * t == slot, piece, 0.0)
        rows.append(
            jnp.concatenate(
                [sums[s // 2][:, (s % 2) * HALF : (s % 2) * HALF + M] for s in range(KC)], axis=1
            )
        )
    block = QUAD * side
    for b in range(ROWS // QUAD):
        at = pl.ds(pl.multiple_of(step * (ROWS * side) + b * block, block), block)
        for g in range(parts):
            part[g, at] = jnp.concatenate(
                [row[g * side : (g + 1) * side] for row in rows[b * QUAD : (b + 1) * QUAD]], axis=0
            )

    @pl.when(step % per == per - 1)
    def _():
        first(step // per).start()
        second(step // per).start()

    @pl.when((step % per == per // 2) & (step >= per))
    def _():
        relay(step // per - 1)

    @pl.when(step == steps - 1)
    def _():
        relay(chunks - 1)
        for q in range(chunks):
            finish(q)

        @pl.loop(1, count)
        def _(d):
            packed(d)
            for copy in send(d):
                copy.start()

        packed(0)
        out_ref[...] = placed(lab_ref[wide], pk[0])

        @pl.loop(1, count)
        def _(d):
            for copy in send(d):
                copy.wait()
            out_ref[...] += placed(rxl[d], rxw[d])


def coarse_rows(op_blocks, near, own, tiles, swaps, slots, src, lab, parts, chunks=4):
    count_rows, terms, part_rows, _ = op_blocks.shape
    side = M // parts
    count, _, height = lab.shape
    steps = count_rows // ROWS
    rows, columns = count_rows * side, KC * M
    vmem = pl.BlockSpec(memory_space=pltpu.VMEM)
    dma = pltpu.SemaphoreType.DMA
    return pl.pallas_call(
        functools.partial(coarse_kernel, count, parts, terms, steps, chunks),
        out_shape=jax.ShapeDtypeStruct((AGG_DEV * side, columns), F32),
        grid_spec=pltpu.PrefetchScalarGridSpec(
            num_scalar_prefetch=3,
            grid=(steps,),
            in_specs=[
                pl.BlockSpec((ROWS, terms, part_rows, B), lambda i, *_: (i, 0, 0, 0)),
                vmem,
                pl.BlockSpec((ROWS, M, part_rows), lambda i, *_: (i, 0, 0)),
                vmem,
                vmem,
            ],
            out_specs=pl.BlockSpec((AGG_DEV * side, columns), lambda i, *_: (0, 0)),
            scratch_shapes=[
                pltpu.VMEM((parts, rows, columns), F32),
                pltpu.VMEM((2, rows, columns), F32),
                pltpu.VMEM((rows, columns), BF16),
                pltpu.VMEM((rows, columns), BF16),
                pltpu.VMEM((count, height, columns), BF16),
                pltpu.VMEM((count, height, columns), BF16),
                pltpu.VMEM((count, 1, height), I32),
                pltpu.VMEM((rows, columns), BF16),
                dma((3, chunks)), dma((3, chunks)),
                dma((count,)), dma((count,)), dma((count,)), dma((count,)),
            ],
        ),
        compiler_params=pltpu.CompilerParams(
            collective_id=0, has_side_effects=True, vmem_limit_bytes=48 << 20
        ),
    )(tiles, swaps, slots, op_blocks, near, own, src, lab)


def routes(owner, local, count, capacity, side):
    rows = owner.shape[0]
    index = jnp.arange(rows, dtype=I32)
    earlier = (owner[:, None] == owner[None, :]) & (index[None, :] < index[:, None])
    rank = jnp.sum(earlier.astype(I32), axis=1)
    height = -(-capacity * side // 16) * 16
    place = jnp.arange(height, dtype=I32)
    wanted = jnp.arange(count, dtype=I32)[:, None] * capacity + place[None, :] // side
    wanted = jnp.where(place[None, :] < capacity * side, wanted, -1)
    match = wanted[:, :, None] == (owner * capacity + rank)[None, None, :]
    filled = jnp.any(match, axis=2)
    inner = place[None, :] % side

    def spread(values):
        picked = jnp.sum(jnp.where(match, values[None, None, :], 0), axis=2)
        return jnp.where(filled, picked * side + inner, -1)

    return spread(index)[:, :, None], spread(local)[:, None, :]


def on_device(op_blocks, prolong, col_index, slot_index, dest_owner, dest_local):
    count_rows, _, part_rows, _ = op_blocks.shape
    count = lax.axis_size("wide")
    parts = lax.axis_size("narrow")
    wide_pos = lax.axis_index("wide")
    capacity = max(2, 2 * count_rows // count)
    side = M // parts
    src, lab = routes(dest_owner[:, 0], dest_local, count, capacity, side)
    pairs = count_rows // 2
    blocks = prolong.reshape(count_rows, part_rows, M)
    gap = jnp.zeros((pairs, part_rows, HALF - M), BF16)
    paired = jnp.concatenate([blocks[:pairs], gap, blocks[pairs:], gap], axis=2)
    near = gathered(paired, count, parts)
    cols = (col_index - wide_pos * count_rows + count_rows).reshape(-1)
    slots = slot_index.reshape(-1)
    inner = cols % count_rows
    tiles = cols // count_rows * pairs + inner % pairs
    swaps = (inner // pairs + slots) % 2
    coarse = coarse_rows(
        op_blocks, near, blocks.swapaxes(1, 2), tiles, swaps, slots, src, lab, parts
    )
    return coarse.reshape(AGG_DEV, side, KC * M)


def solution(mesh):
    in_specs = (
        P("wide", None, "narrow", None),
        P("wide", "narrow"),
        P("wide", None),
        P("wide", None),
        P("wide", None),
        P("wide"),
    )
    out_specs = P("wide", "narrow", None)
    return jax.shard_map(
        on_device, mesh=mesh, in_specs=in_specs, out_specs=out_specs, check_vma=False
    )
```

```python
import functools

import jax
import jax.numpy as jnp
from jax import lax
from jax.experimental import pallas as pl
from jax.experimental.pallas import tpu as pltpu
from jax.sharding import PartitionSpec as P

B = 192
M = 48
KC = 8
AGG_DEV = 16
HALF = 64
QUAD = 4
ROWS = 8
MESH = pl.DeviceIdType.MESH
F32 = jnp.float32
BF16 = jnp.bfloat16
I32 = jnp.int32


def gather_kernel(count, parts, chunks, own_ref, near_ref, ss, rs, keep_sem):
    wide = lax.axis_index("wide")
    me = lax.axis_index("narrow")
    near = me + 1 - 2 * (me % 2)
    far = (me + 2) % parts
    pairs, depth, _ = own_ref.shape
    piece = pairs // chunks
    first, last = wide == 0, wide == count - 1
    has = {0: jnp.logical_not(first), 1: None, 2: jnp.logical_not(last)}
    barrier = pltpu.get_barrier_semaphore()

    def when(cond, fn):
        fn() if cond is None else pl.when(cond)(fn)

    def hello(where):
        pl.semaphore_signal(barrier, inc=1, device_id=where, device_id_type=MESH)

    hello((wide, near))
    hello((wide, far))
    when(has[0], lambda: hello((wide - 1, me)))
    when(has[2], lambda: hello((wide + 1, me)))
    sides = (wide + count - 1) // count + (2 * count - 2 - wide) // count
    pl.semaphore_wait(barrier, 2 + sides)

    def place(slot, part, c):
        return near_ref.at[pl.ds(slot * pairs + c * piece, piece), pl.ds(part * depth, depth)]

    def remote(slot, kind, c, target, source, part, sent=None):
        return pltpu.make_async_remote_copy(
            src_ref=source,
            dst_ref=place(slot, part, c),
            send_sem=ss.at[slot, kind if sent is None else sent, c],
            recv_sem=rs.at[slot, kind, c],
            device_id=target,
            device_id_type=MESH,
        )

    def mine(c):
        return own_ref.at[pl.ds(c * piece, piece)]

    def direct(slot, c):
        target = (wide + 1 if slot == 0 else wide - 1, me)
        return remote(slot, 0, c, target, mine(c), me)

    def held(slot, c):
        return mine(c) if slot == 1 else place(slot, me, c)

    def to_near(slot, c):
        return remote(slot, 1, c, (wide, near), held(slot, c), me)

    def to_far(slot, c):
        return remote(slot, 2, c, (wide, far), held(slot, c), me)

    def onward(slot, c):
        return remote(slot, 3, c, (wide, near), place(slot, far, c), far)

    keep = pltpu.make_async_copy(
        own_ref, near_ref.at[pl.ds(pairs, pairs), pl.ds(me * depth, depth)], keep_sem
    )
    for c in range(chunks):
        to_far(1, c).start()
        when(has[2], lambda: direct(0, c).start())
        when(has[0], lambda: direct(2, c).start())
        to_near(1, c).start()
    keep.start()

    def across(slot, c):
        target = (wide + 1 if slot == 0 else wide - 1, me)
        return remote(slot, 2, c, target, place(1, far, c), far, sent=4)

    twin = {0: has[2] & (wide % 2 == 0), 2: wide % 2 == 1}
    paired = {0: wide % 2 == 1, 2: has[2] & (wide % 2 == 0)}
    detour = [c for c in range(chunks) if c < chunks // 2]

    def spread(slot, c):
        direct(slot, c).wait_recv()
        to_near(slot, c).start()
        if c in detour:
            pl.when(jnp.logical_not(paired[slot]))(lambda: to_far(slot, c).start())
        else:
            to_far(slot, c).start()

    def forward(slot, c):
        to_far(slot, c).wait_recv()
        onward(slot, c).start()
        if slot == 1 and c in detour:
            for there in (0, 2):
                pl.when(twin[there])(lambda: across(there, c).start())

    for c in range(chunks):
        forward(1, c)
        when(has[0], lambda: spread(0, c))
        when(has[2], lambda: spread(2, c))
    for c in range(chunks):
        when(has[0], lambda: forward(0, c))
        when(has[2], lambda: forward(2, c))

    def drain(slot):
        for c in range(chunks):
            to_near(slot, c).wait()
            if slot != 1 and c in detour:
                pl.when(jnp.logical_not(paired[slot]))(lambda: to_far(slot, c).wait_send())
            else:
                to_far(slot, c).wait_send()
            onward(slot, c).wait()

    for slot in range(3):
        when(has[slot], lambda: drain(slot))
    for c in detour:
        for there in (0, 2):
            pl.when(twin[there])(lambda: across(there, c).wait_send())
    for c in range(chunks):
        when(has[2], lambda: direct(0, c).wait_send())
        when(has[0], lambda: direct(2, c).wait_send())
    keep.wait()


def gathered(own, count, parts, chunks=4):
    pairs, depth, lanes = own.shape
    hbm = pl.BlockSpec(memory_space=pl.ANY)
    sems = pltpu.SemaphoreType.DMA((3, 5, chunks))
    return pl.pallas_call(
        functools.partial(gather_kernel, count, parts, chunks),
        out_shape=jax.ShapeDtypeStruct((3 * pairs, parts * depth, lanes), BF16),
        in_specs=[hbm],
        out_specs=hbm,
        scratch_shapes=[sems, sems, pltpu.SemaphoreType.DMA],
        compiler_params=pltpu.CompilerParams(collective_id=1, has_side_effects=True),
    )(own)


def coarse_kernel(
    count, parts, terms, steps, chunks,
    tile_ref, swap_ref, slot_ref, op_ref, near_ref, own_ref, src_ref, lab_ref, out_ref,
    part, rx1, tx2, rx2, pk, rxw, rxl, summed, ns, nr, ws, wr, ls, lr,
):
    step = pl.program_id(0)
    wide = lax.axis_index("wide")
    me = lax.axis_index("narrow")
    near = me + 1 - 2 * (me % 2)
    far = (me + 2) % parts
    cross = (near + 2) % parts
    side = M // parts
    per = steps // chunks
    height = pk.shape[1]
    chunk_rows = summed.shape[0] // chunks

    def remote(src, dst, s, r, target):
        return pltpu.make_async_remote_copy(
            src_ref=src, dst_ref=dst, send_sem=s, recv_sem=r, device_id=target, device_id_type=MESH
        )

    def rows_of(q):
        return pl.ds(pl.multiple_of(q * chunk_rows, chunk_rows), chunk_rows)

    def first(q):
        r = rows_of(q)
        return remote(part.at[cross, r], rx1.at[1, r], ns.at[0, q], nr.at[0, q], (wide, near))

    def second(q):
        r = rows_of(q)
        return remote(part.at[near, r], rx1.at[0, r], ns.at[1, q], nr.at[1, q], (wide, near))

    def third(q):
        r = rows_of(q)
        return remote(tx2.at[r], rx2.at[r], ns.at[2, q], nr.at[2, q], (wide, far))

    def relay(q):
        r = rows_of(q)
        first(q).wait()
        tx2[r] = (part[far, r] + rx1[1, r]).astype(BF16)
        third(q).start()

    def finish(q):
        r = rows_of(q)
        second(q).wait()
        third(q).wait()
        summed[r] = (part[me, r] + rx1[0, r] + rx2[r].astype(F32)).astype(BF16)

    def send(d):
        other = (wide + d) % count
        return (
            remote(pk.at[d], rxw.at[d], ws.at[d], wr.at[d], (other, me)),
            remote(lab_ref.at[other], rxl.at[d], ls.at[d], lr.at[d], (other, me)),
        )

    def packed(d):
        lanes = lax.broadcasted_iota(I32, (height, summed.shape[0]), 1)
        pick = (src_ref[(wide + d) % count] == lanes).astype(F32).astype(BF16)
        pk[d] = jnp.dot(pick, summed[...], preferred_element_type=F32).astype(BF16)

    def placed(labels, rows):
        places = lax.broadcasted_iota(I32, (out_ref.shape[0], height), 0)
        pick = (labels == places).astype(F32).astype(BF16)
        return jnp.dot(pick, rows, preferred_element_type=F32)

    @pl.when(step == 0)
    def _():
        barrier = pltpu.get_barrier_semaphore()
        pl.semaphore_signal(barrier, inc=1, device_id=(wide, near), device_id_type=MESH)
        pl.semaphore_signal(barrier, inc=1, device_id=(wide, far), device_id_type=MESH)

        @pl.loop(1, count)
        def _(d):
            pl.semaphore_signal(
                barrier, inc=1, device_id=((wide + d) % count, me), device_id_type=MESH
            )

        pl.semaphore_wait(barrier, count + 1)

    lane_half = lax.broadcasted_iota(I32, (1, 2 * HALF), 1) // HALF
    applied = []
    for j in range(ROWS):
        base = (step * ROWS + j) * terms
        for k in range(0, terms, 2):
            tiles = jnp.concatenate(
                [near_ref[tile_ref[base + k]], near_ref[tile_ref[base + k + 1]]], axis=1
            )
            stacked = op_ref[j, k : k + 2].reshape(-1, B)
            both = jnp.dot(stacked, tiles, preferred_element_type=F32)
            depth = both.shape[0] // 2
            applied.append(both[:depth, : 2 * HALF].astype(BF16))
            applied.append(both[depth:, 2 * HALF :].astype(BF16))
    rows = []
    for j in range(ROWS):
        base = (step * ROWS + j) * terms
        held = jnp.concatenate(applied[j * terms : (j + 1) * terms], axis=1)
        projected = jnp.dot(own_ref[j], held, preferred_element_type=F32)
        sums = [jnp.zeros((M, 2 * HALF), F32) for _ in range(KC // 2)]
        for k in range(terms):
            slot = slot_ref[base + k]
            piece = projected[:, k * 2 * HALF : (k + 1) * 2 * HALF]
            piece = jnp.where(swap_ref[base + k] == 1, pltpu.roll(piece, HALF, 1), piece)
            for t in range(KC // 2):
                sums[t] = sums[t] + jnp.where(lane_half + 2 * t == slot, piece, 0.0)
        rows.append(
            jnp.concatenate(
                [sums[s // 2][:, (s % 2) * HALF : (s % 2) * HALF + M] for s in range(KC)], axis=1
            )
        )
    block = QUAD * side
    for b in range(ROWS // QUAD):
        at = pl.ds(pl.multiple_of(step * (ROWS * side) + b * block, block), block)
        for g in range(parts):
            part[g, at] = jnp.concatenate(
                [row[g * side : (g + 1) * side] for row in rows[b * QUAD : (b + 1) * QUAD]], axis=0
            )

    @pl.when(step % per == per - 1)
    def _():
        first(step // per).start()
        second(step // per).start()

    @pl.when((step % per == per // 2) & (step >= per))
    def _():
        relay(step // per - 1)

    lag = 3

    @pl.when((step % per == per - 1) & (step >= lag * per))
    def _():
        finish(step // per - lag)

    @pl.when(step == steps - 1)
    def _():
        relay(chunks - 1)
        for q in range(chunks - lag, chunks):
            finish(q)

        def turn(i):
            return 1 + (i + count // 2 - 1) % (count - 1)

        @pl.loop(0, count - 1)
        def _(i):
            d = turn(i)
            packed(d)
            for copy in send(d):
                copy.start()

        packed(0)
        out_ref[...] = placed(lab_ref[wide], pk[0])

        @pl.loop(0, count - 1)
        def _(i):
            d = turn(i)
            for copy in send(d):
                copy.wait()
            out_ref[...] += placed(rxl[d], rxw[d])


def coarse_rows(op_blocks, near, own, tiles, swaps, slots, src, lab, parts, chunks=8):
    count_rows, terms, part_rows, _ = op_blocks.shape
    side = M // parts
    count, _, height = lab.shape
    steps = count_rows // ROWS
    rows, columns = count_rows * side, KC * M
    vmem = pl.BlockSpec(memory_space=pltpu.VMEM)
    dma = pltpu.SemaphoreType.DMA
    return pl.pallas_call(
        functools.partial(coarse_kernel, count, parts, terms, steps, chunks),
        out_shape=jax.ShapeDtypeStruct((AGG_DEV * side, columns), F32),
        grid_spec=pltpu.PrefetchScalarGridSpec(
            num_scalar_prefetch=3,
            grid=(steps,),
            in_specs=[
                pl.BlockSpec((ROWS, terms, part_rows, B), lambda i, *_: (i, 0, 0, 0)),
                vmem,
                pl.BlockSpec((ROWS, M, part_rows), lambda i, *_: (i, 0, 0)),
                vmem,
                vmem,
            ],
            out_specs=pl.BlockSpec((AGG_DEV * side, columns), lambda i, *_: (0, 0)),
            scratch_shapes=[
                pltpu.VMEM((parts, rows, columns), F32),
                pltpu.VMEM((2, rows, columns), F32),
                pltpu.VMEM((rows, columns), BF16),
                pltpu.VMEM((rows, columns), BF16),
                pltpu.VMEM((count, height, columns), BF16),
                pltpu.VMEM((count, height, columns), BF16),
                pltpu.VMEM((count, 1, height), I32),
                pltpu.VMEM((rows, columns), BF16),
                dma((3, chunks)), dma((3, chunks)),
                dma((count,)), dma((count,)), dma((count,)), dma((count,)),
            ],
        ),
        compiler_params=pltpu.CompilerParams(
            collective_id=0, has_side_effects=True, vmem_limit_bytes=48 << 20
        ),
    )(tiles, swaps, slots, op_blocks, near, own, src, lab)


def routes(owner, local, count, capacity, side):
    rows = owner.shape[0]
    index = jnp.arange(rows, dtype=I32)
    earlier = (owner[:, None] == owner[None, :]) & (index[None, :] < index[:, None])
    rank = jnp.sum(earlier.astype(I32), axis=1)
    height = -(-capacity * side // 16) * 16
    place = jnp.arange(height, dtype=I32)
    wanted = jnp.arange(count, dtype=I32)[:, None] * capacity + place[None, :] // side
    wanted = jnp.where(place[None, :] < capacity * side, wanted, -1)
    match = wanted[:, :, None] == (owner * capacity + rank)[None, None, :]
    filled = jnp.any(match, axis=2)
    inner = place[None, :] % side

    def spread(values):
        picked = jnp.sum(jnp.where(match, values[None, None, :], 0), axis=2)
        return jnp.where(filled, picked * side + inner, -1)

    return spread(index)[:, :, None], spread(local)[:, None, :]


def on_device(op_blocks, prolong, col_index, slot_index, dest_owner, dest_local):
    count_rows, _, part_rows, _ = op_blocks.shape
    count = lax.axis_size("wide")
    parts = lax.axis_size("narrow")
    wide_pos = lax.axis_index("wide")
    capacity = max(2, 2 * count_rows // count)
    side = M // parts
    src, lab = routes(dest_owner[:, 0], dest_local, count, capacity, side)
    pairs = count_rows // 2
    blocks = prolong.reshape(count_rows, part_rows, M)
    gap = jnp.zeros((pairs, part_rows, HALF - M), BF16)
    paired = jnp.concatenate([blocks[:pairs], gap, blocks[pairs:], gap], axis=2)
    near = gathered(paired, count, parts)
    cols = (col_index - wide_pos * count_rows + count_rows).reshape(-1)
    slots = slot_index.reshape(-1)
    inner = cols % count_rows
    tiles = cols // count_rows * pairs + inner % pairs
    swaps = (inner // pairs + slots) % 2
    coarse = coarse_rows(
        op_blocks, near, blocks.swapaxes(1, 2), tiles, swaps, slots, src, lab, parts
    )
    return coarse.reshape(AGG_DEV, side, KC * M)


def solution(mesh):
    in_specs = (
        P("wide", None, "narrow", None),
        P("wide", "narrow"),
        P("wide", None),
        P("wide", None),
        P("wide", None),
        P("wide"),
    )
    out_specs = P("wide", "narrow", None)
    return jax.shard_map(
        on_device, mesh=mesh, in_specs=in_specs, out_specs=out_specs, check_vma=False
    )
```

```python
import functools

import jax
import jax.numpy as jnp
from jax import lax
from jax.experimental import pallas as pl
from jax.experimental.pallas import tpu as pltpu
from jax.sharding import PartitionSpec as P

B = 192
M = 48
KC = 8
AGG_DEV = 16
HALF = 64
QUAD = 4
ROWS = 8
MESH = pl.DeviceIdType.MESH
F32 = jnp.float32
BF16 = jnp.bfloat16
I32 = jnp.int32


def gather_kernel(count, parts, chunks, own_ref, near_ref, ss, rs, keep_sem):
    wide = lax.axis_index("wide")
    me = lax.axis_index("narrow")
    near = me + 1 - 2 * (me % 2)
    far = (me + 2) % parts
    pairs, depth, _ = own_ref.shape
    piece = pairs // chunks
    first, last = wide == 0, wide == count - 1
    has = {0: jnp.logical_not(first), 1: None, 2: jnp.logical_not(last)}
    barrier = pltpu.get_barrier_semaphore()

    def when(cond, fn):
        fn() if cond is None else pl.when(cond)(fn)

    def hello(where):
        pl.semaphore_signal(barrier, inc=1, device_id=where, device_id_type=MESH)

    hello((wide, near))
    hello((wide, far))
    when(has[0], lambda: hello((wide - 1, me)))
    when(has[2], lambda: hello((wide + 1, me)))
    sides = (wide + count - 1) // count + (2 * count - 2 - wide) // count
    pl.semaphore_wait(barrier, 2 + sides)

    def place(slot, part, c):
        return near_ref.at[pl.ds(slot * pairs + c * piece, piece), pl.ds(part * depth, depth)]

    def remote(slot, kind, c, target, source, part, sent=None):
        return pltpu.make_async_remote_copy(
            src_ref=source,
            dst_ref=place(slot, part, c),
            send_sem=ss.at[slot, kind if sent is None else sent, c],
            recv_sem=rs.at[slot, kind, c],
            device_id=target,
            device_id_type=MESH,
        )

    def mine(c):
        return own_ref.at[pl.ds(c * piece, piece)]

    def direct(slot, c):
        target = (wide + 1 if slot == 0 else wide - 1, me)
        return remote(slot, 0, c, target, mine(c), me)

    def held(slot, c):
        return mine(c) if slot == 1 else place(slot, me, c)

    def to_near(slot, c):
        return remote(slot, 1, c, (wide, near), held(slot, c), me)

    def to_far(slot, c):
        return remote(slot, 2, c, (wide, far), held(slot, c), me)

    def onward(slot, c):
        return remote(slot, 3, c, (wide, near), place(slot, far, c), far)

    keep = pltpu.make_async_copy(
        own_ref, near_ref.at[pl.ds(pairs, pairs), pl.ds(me * depth, depth)], keep_sem
    )
    for c in range(chunks):
        to_far(1, c).start()
        when(has[2], lambda: direct(0, c).start())
        when(has[0], lambda: direct(2, c).start())
        to_near(1, c).start()
    keep.start()

    def across(slot, c):
        target = (wide + 1 if slot == 0 else wide - 1, me)
        return remote(slot, 2, c, target, place(1, far, c), far, sent=4)

    twin = {0: has[2] & (wide % 2 == 0), 2: wide % 2 == 1}
    paired = {0: wide % 2 == 1, 2: has[2] & (wide % 2 == 0)}
    detour = [c for c in range(chunks) if c < chunks // 2]

    def spread(slot, c):
        direct(slot, c).wait_recv()
        to_near(slot, c).start()
        if c in detour:
            pl.when(jnp.logical_not(paired[slot]))(lambda: to_far(slot, c).start())
        else:
            to_far(slot, c).start()

    def forward(slot, c):
        to_far(slot, c).wait_recv()
        onward(slot, c).start()
        if slot == 1 and c in detour:
            for there in (0, 2):
                pl.when(twin[there])(lambda: across(there, c).start())

    for c in range(chunks):
        forward(1, c)
        when(has[0], lambda: spread(0, c))
        when(has[2], lambda: spread(2, c))
    for c in range(chunks):
        when(has[0], lambda: forward(0, c))
        when(has[2], lambda: forward(2, c))

    def drain(slot):
        for c in range(chunks):
            to_near(slot, c).wait()
            if slot != 1 and c in detour:
                pl.when(jnp.logical_not(paired[slot]))(lambda: to_far(slot, c).wait_send())
            else:
                to_far(slot, c).wait_send()
            onward(slot, c).wait()

    for slot in range(3):
        when(has[slot], lambda: drain(slot))
    for c in detour:
        for there in (0, 2):
            pl.when(twin[there])(lambda: across(there, c).wait_send())
    for c in range(chunks):
        when(has[2], lambda: direct(0, c).wait_send())
        when(has[0], lambda: direct(2, c).wait_send())
    keep.wait()


def gathered(own, count, parts, chunks=4):
    pairs, depth, lanes = own.shape
    hbm = pl.BlockSpec(memory_space=pl.ANY)
    sems = pltpu.SemaphoreType.DMA((3, 5, chunks))
    return pl.pallas_call(
        functools.partial(gather_kernel, count, parts, chunks),
        out_shape=jax.ShapeDtypeStruct((3 * pairs, parts * depth, lanes), BF16),
        in_specs=[hbm],
        out_specs=hbm,
        scratch_shapes=[sems, sems, pltpu.SemaphoreType.DMA],
        compiler_params=pltpu.CompilerParams(collective_id=1, has_side_effects=True),
    )(own)


def coarse_kernel(
    count, parts, terms, steps, chunks,
    tile_ref, swap_ref, slot_ref, op_ref, near_ref, own_ref, key_ref, out_ref,
    part, rx1, tx2, rx2, pk, rxw, rxk, summed, rxs, ns, nr, ys, yr, ws, wr, ks,
):
    step = pl.program_id(0)
    wide = lax.axis_index("wide")
    me = lax.axis_index("narrow")
    near = me + 1 - 2 * (me % 2)
    far = (me + 2) % parts
    cross = (near + 2) % parts
    side = M // parts
    per = steps // chunks
    half = count // 2
    twin = wide + 1 - 2 * (wide % 2)
    height = pk.shape[1]
    chunk_rows = summed.shape[0] // chunks

    def remote(src, dst, s, r, target):
        return pltpu.make_async_remote_copy(
            src_ref=src, dst_ref=dst, send_sem=s, recv_sem=r, device_id=target, device_id_type=MESH
        )

    def rows_of(q):
        return pl.ds(pl.multiple_of(q * chunk_rows, chunk_rows), chunk_rows)

    def first(q):
        r = rows_of(q)
        return remote(part.at[cross, r], rx1.at[1, r], ns.at[0, q], nr.at[0, q], (wide, near))

    def second(q):
        r = rows_of(q)
        return remote(part.at[near, r], rx1.at[0, r], ns.at[1, q], nr.at[1, q], (wide, near))

    def third(q):
        r = rows_of(q)
        return remote(tx2.at[r], rx2.at[r], ns.at[2, q], nr.at[2, q], (wide, far))

    def relay(q):
        r = rows_of(q)
        first(q).wait()
        tx2[r] = (part[far, r] + rx1[1, r]).astype(BF16)
        third(q).start()

    def finish(q):
        r = rows_of(q)
        second(q).wait()
        third(q).wait()
        summed[r] = (part[me, r] + rx1[0, r] + rx2[r].astype(F32)).astype(BF16)

    def fourth(q):
        r = rows_of(q)
        return remote(summed.at[r], rxs.at[r], ys.at[q], yr.at[q], (twin, me))

    def keys():
        return remote(key_ref, rxk, ks.at[0], ks.at[1], (twin, me))

    def send(d):
        return remote(pk.at[d], rxw.at[d], ws.at[d], wr.at[d], ((wide + 2 * d) % count, me))

    def dense(owner):
        places = lax.broadcasted_iota(I32, (height, summed.shape[0]), 0) + owner * height
        ours = (key_ref[...] == places).astype(F32).astype(BF16)
        theirs = (rxk[...] == places).astype(F32).astype(BF16)
        return jnp.dot(ours, summed[...], preferred_element_type=F32) + jnp.dot(
            theirs, rxs[...], preferred_element_type=F32
        )

    @pl.when(step == 0)
    def _():
        barrier = pltpu.get_barrier_semaphore()
        pl.semaphore_signal(barrier, inc=1, device_id=(wide, near), device_id_type=MESH)
        pl.semaphore_signal(barrier, inc=1, device_id=(wide, far), device_id_type=MESH)

        pl.semaphore_signal(barrier, inc=1, device_id=(twin, me), device_id_type=MESH)

        @pl.loop(1, half)
        def _(d):
            pl.semaphore_signal(
                barrier, inc=1, device_id=((wide + 2 * d) % count, me), device_id_type=MESH
            )

        pl.semaphore_wait(barrier, half + 2)
        keys().start()

    lane_half = lax.broadcasted_iota(I32, (1, 2 * HALF), 1) // HALF
    applied = []
    for j in range(ROWS):
        base = (step * ROWS + j) * terms
        for k in range(0, terms, 2):
            tiles = jnp.concatenate(
                [near_ref[tile_ref[base + k]], near_ref[tile_ref[base + k + 1]]], axis=1
            )
            stacked = op_ref[j, k : k + 2].reshape(-1, B)
            both = jnp.dot(stacked, tiles, preferred_element_type=F32)
            depth = both.shape[0] // 2
            applied.append(both[:depth, : 2 * HALF].astype(BF16))
            applied.append(both[depth:, 2 * HALF :].astype(BF16))
    rows = []
    for j in range(ROWS):
        base = (step * ROWS + j) * terms
        held = jnp.concatenate(applied[j * terms : (j + 1) * terms], axis=1)
        projected = jnp.dot(own_ref[j], held, preferred_element_type=F32)
        sums = [jnp.zeros((M, 2 * HALF), F32) for _ in range(KC // 2)]
        for k in range(terms):
            slot = slot_ref[base + k]
            piece = projected[:, k * 2 * HALF : (k + 1) * 2 * HALF]
            piece = jnp.where(swap_ref[base + k] == 1, pltpu.roll(piece, HALF, 1), piece)
            for t in range(KC // 2):
                sums[t] = sums[t] + jnp.where(lane_half + 2 * t == slot, piece, 0.0)
        rows.append(
            jnp.concatenate(
                [sums[s // 2][:, (s % 2) * HALF : (s % 2) * HALF + M] for s in range(KC)], axis=1
            )
        )
    block = QUAD * side
    for b in range(ROWS // QUAD):
        at = pl.ds(pl.multiple_of(step * (ROWS * side) + b * block, block), block)
        for g in range(parts):
            part[g, at] = jnp.concatenate(
                [row[g * side : (g + 1) * side] for row in rows[b * QUAD : (b + 1) * QUAD]], axis=0
            )

    @pl.when(step % per == per - 1)
    def _():
        first(step // per).start()
        second(step // per).start()

    @pl.when((step % per == per // 2) & (step >= per))
    def _():
        relay(step // per - 1)

    lag = 2

    @pl.when((step % per == per - 1) & (step >= lag * per))
    def _():
        finish(step // per - lag)
        fourth(step // per - lag).start()

    @pl.when(step == steps - 1)
    def _():
        relay(chunks - 1)
        for q in range(chunks - lag, chunks):
            finish(q)
            fourth(q).start()
        keys().wait()
        for q in range(chunks):
            fourth(q).wait()

        def turn(i):
            return 1 + (i + half // 2 - 1) % (half - 1)

        @pl.loop(0, half - 1)
        def _(i):
            d = turn(i)
            pk[d] = dense((wide + 2 * d) % count).astype(BF16)
            send(d).start()

        out_ref[...] = dense(wide)

        @pl.loop(0, half - 1)
        def _(i):
            d = turn(i)
            send(d).wait()
            out_ref[...] += rxw[d].astype(F32)


def coarse_rows(op_blocks, near, own, tiles, swaps, slots, keys, count, parts, chunks=8):
    count_rows, terms, part_rows, _ = op_blocks.shape
    side = M // parts
    height = AGG_DEV * side
    steps = count_rows // ROWS
    rows, columns = count_rows * side, KC * M
    vmem = pl.BlockSpec(memory_space=pltpu.VMEM)
    dma = pltpu.SemaphoreType.DMA
    return pl.pallas_call(
        functools.partial(coarse_kernel, count, parts, terms, steps, chunks),
        out_shape=jax.ShapeDtypeStruct((AGG_DEV * side, columns), F32),
        grid_spec=pltpu.PrefetchScalarGridSpec(
            num_scalar_prefetch=3,
            grid=(steps,),
            in_specs=[
                pl.BlockSpec((ROWS, terms, part_rows, B), lambda i, *_: (i, 0, 0, 0)),
                vmem,
                pl.BlockSpec((ROWS, M, part_rows), lambda i, *_: (i, 0, 0)),
                vmem,
            ],
            out_specs=pl.BlockSpec((AGG_DEV * side, columns), lambda i, *_: (0, 0)),
            scratch_shapes=[
                pltpu.VMEM((parts, rows, columns), F32),
                pltpu.VMEM((2, rows, columns), F32),
                pltpu.VMEM((rows, columns), BF16),
                pltpu.VMEM((rows, columns), BF16),
                pltpu.VMEM((count // 2, height, columns), BF16),
                pltpu.VMEM((count // 2, height, columns), BF16),
                pltpu.VMEM((1, rows), I32),
                pltpu.VMEM((rows, columns), BF16),
                pltpu.VMEM((rows, columns), BF16),
                dma((3, chunks)), dma((3, chunks)), dma((chunks,)), dma((chunks,)),
                dma((count // 2,)), dma((count // 2,)), dma((2,)),
            ],
        ),
        compiler_params=pltpu.CompilerParams(
            collective_id=0, has_side_effects=True, vmem_limit_bytes=48 << 20
        ),
    )(tiles, swaps, slots, op_blocks, near, own, keys)


def on_device(op_blocks, prolong, col_index, slot_index, dest_owner, dest_local):
    count_rows, _, part_rows, _ = op_blocks.shape
    count = lax.axis_size("wide")
    parts = lax.axis_size("narrow")
    wide_pos = lax.axis_index("wide")
    side = M // parts
    goal = (dest_owner[:, 0] * AGG_DEV + dest_local) * side
    keys = (goal[:, None] + jnp.arange(side, dtype=I32)[None, :]).reshape(1, -1)
    pairs = count_rows // 2
    blocks = prolong.reshape(count_rows, part_rows, M)
    gap = jnp.zeros((pairs, part_rows, HALF - M), BF16)
    paired = jnp.concatenate([blocks[:pairs], gap, blocks[pairs:], gap], axis=2)
    near = gathered(paired, count, parts)
    cols = (col_index - wide_pos * count_rows + count_rows).reshape(-1)
    slots = slot_index.reshape(-1)
    inner = cols % count_rows
    tiles = cols // count_rows * pairs + inner % pairs
    swaps = (inner // pairs + slots) % 2
    coarse = coarse_rows(
        op_blocks, near, blocks.swapaxes(1, 2), tiles, swaps, slots, keys, count, parts
    )
    return coarse.reshape(AGG_DEV, side, KC * M)


def solution(mesh):
    in_specs = (
        P("wide", None, "narrow", None),
        P("wide", "narrow"),
        P("wide", None),
        P("wide", None),
        P("wide", None),
        P("wide"),
    )
    out_specs = P("wide", "narrow", None)
    return jax.shard_map(
        on_device, mesh=mesh, in_specs=in_specs, out_specs=out_specs, check_vma=False
    )
```

```python
import functools

import jax
import jax.numpy as jnp
from jax import lax
from jax.experimental import pallas as pl
from jax.experimental.pallas import tpu as pltpu
from jax.sharding import PartitionSpec as P

B = 192
M = 48
KC = 8
AGG_DEV = 16
HALF = 64
QUAD = 4
ROWS = 8
MESH = pl.DeviceIdType.MESH
F32 = jnp.float32
BF16 = jnp.bfloat16
I32 = jnp.int32


def gather_kernel(count, parts, chunks, own_ref, near_ref, ss, rs, keep_sem):
    wide = lax.axis_index("wide")
    me = lax.axis_index("narrow")
    near = me + 1 - 2 * (me % 2)
    far = (me + 2) % parts
    pairs, depth, _ = own_ref.shape
    piece = pairs // chunks
    first, last = wide == 0, wide == count - 1
    has = {0: jnp.logical_not(first), 1: None, 2: jnp.logical_not(last)}
    barrier = pltpu.get_barrier_semaphore()

    def when(cond, fn):
        fn() if cond is None else pl.when(cond)(fn)

    def hello(where):
        pl.semaphore_signal(barrier, inc=1, device_id=where, device_id_type=MESH)

    hello((wide, near))
    hello((wide, far))
    when(has[0], lambda: hello((wide - 1, me)))
    when(has[2], lambda: hello((wide + 1, me)))
    sides = (wide + count - 1) // count + (2 * count - 2 - wide) // count
    pl.semaphore_wait(barrier, 2 + sides)

    def place(slot, part, c):
        return near_ref.at[pl.ds(slot * pairs + c * piece, piece), pl.ds(part * depth, depth)]

    def remote(slot, kind, c, target, source, part, sent=None):
        return pltpu.make_async_remote_copy(
            src_ref=source,
            dst_ref=place(slot, part, c),
            send_sem=ss.at[slot, kind if sent is None else sent, c],
            recv_sem=rs.at[slot, kind, c],
            device_id=target,
            device_id_type=MESH,
        )

    def mine(c):
        return own_ref.at[pl.ds(c * piece, piece)]

    def direct(slot, c):
        target = (wide + 1 if slot == 0 else wide - 1, me)
        return remote(slot, 0, c, target, mine(c), me)

    def held(slot, c):
        return mine(c) if slot == 1 else place(slot, me, c)

    def to_near(slot, c):
        return remote(slot, 1, c, (wide, near), held(slot, c), me)

    def to_far(slot, c):
        return remote(slot, 2, c, (wide, far), held(slot, c), me)

    def onward(slot, c):
        return remote(slot, 3, c, (wide, near), place(slot, far, c), far)

    keep = pltpu.make_async_copy(
        own_ref, near_ref.at[pl.ds(pairs, pairs), pl.ds(me * depth, depth)], keep_sem
    )
    for c in range(chunks):
        to_far(1, c).start()
        when(has[2], lambda: direct(0, c).start())
        when(has[0], lambda: direct(2, c).start())
        to_near(1, c).start()
    keep.start()

    def across(slot, c):
        target = (wide + 1 if slot == 0 else wide - 1, me)
        return remote(slot, 2, c, target, place(1, far, c), far, sent=4)

    twin = {0: has[2] & (wide % 2 == 0), 2: wide % 2 == 1}
    paired = {0: wide % 2 == 1, 2: has[2] & (wide % 2 == 0)}
    detour = [c for c in range(chunks) if c < chunks // 2]

    def spread(slot, c):
        direct(slot, c).wait_recv()
        to_near(slot, c).start()
        if c in detour:
            pl.when(jnp.logical_not(paired[slot]))(lambda: to_far(slot, c).start())
        else:
            to_far(slot, c).start()

    def forward(slot, c):
        to_far(slot, c).wait_recv()
        onward(slot, c).start()
        if slot == 1 and c in detour:
            for there in (0, 2):
                pl.when(twin[there])(lambda: across(there, c).start())

    for c in range(chunks):
        forward(1, c)
        when(has[0], lambda: spread(0, c))
        when(has[2], lambda: spread(2, c))
    for c in range(chunks):
        when(has[0], lambda: forward(0, c))
        when(has[2], lambda: forward(2, c))

    def drain(slot):
        for c in range(chunks):
            to_near(slot, c).wait()
            if slot != 1 and c in detour:
                pl.when(jnp.logical_not(paired[slot]))(lambda: to_far(slot, c).wait_send())
            else:
                to_far(slot, c).wait_send()
            onward(slot, c).wait()

    for slot in range(3):
        when(has[slot], lambda: drain(slot))
    for c in detour:
        for there in (0, 2):
            pl.when(twin[there])(lambda: across(there, c).wait_send())
    for c in range(chunks):
        when(has[2], lambda: direct(0, c).wait_send())
        when(has[0], lambda: direct(2, c).wait_send())
    keep.wait()


def gathered(own, count, parts, chunks=8):
    pairs, depth, lanes = own.shape
    hbm = pl.BlockSpec(memory_space=pl.ANY)
    sems = pltpu.SemaphoreType.DMA((3, 5, chunks))
    return pl.pallas_call(
        functools.partial(gather_kernel, count, parts, chunks),
        out_shape=jax.ShapeDtypeStruct((3 * pairs, parts * depth, lanes), BF16),
        in_specs=[hbm],
        out_specs=hbm,
        scratch_shapes=[sems, sems, pltpu.SemaphoreType.DMA],
        compiler_params=pltpu.CompilerParams(collective_id=1, has_side_effects=True),
    )(own)


def coarse_kernel(
    count, parts, terms, steps, chunks,
    tile_ref, swap_ref, slot_ref, op_ref, near_ref, own_ref, key_ref, out_ref,
    part, rx1, tx2, rx2, pk, rxw, rxk, summed, rxs, ns, nr, ys, yr, ws, wr, ks,
):
    step = pl.program_id(0)
    wide = lax.axis_index("wide")
    me = lax.axis_index("narrow")
    near = me + 1 - 2 * (me % 2)
    far = (me + 2) % parts
    cross = (near + 2) % parts
    side = M // parts
    per = steps // chunks
    half = count // 2
    twin = wide + 1 - 2 * (wide % 2)
    height = pk.shape[1]
    chunk_rows = summed.shape[0] // chunks

    def remote(src, dst, s, r, target):
        return pltpu.make_async_remote_copy(
            src_ref=src, dst_ref=dst, send_sem=s, recv_sem=r, device_id=target, device_id_type=MESH
        )

    def rows_of(q):
        return pl.ds(pl.multiple_of(q * chunk_rows, chunk_rows), chunk_rows)

    def first(q):
        r = rows_of(q)
        return remote(part.at[cross, r], rx1.at[1, r], ns.at[0, q], nr.at[0, q], (wide, near))

    def second(q):
        r = rows_of(q)
        return remote(part.at[near, r], rx1.at[0, r], ns.at[1, q], nr.at[1, q], (wide, near))

    def third(q):
        r = rows_of(q)
        return remote(tx2.at[r], rx2.at[r], ns.at[2, q], nr.at[2, q], (wide, far))

    def relay(q):
        r = rows_of(q)
        first(q).wait()
        tx2[r] = (part[far, r] + rx1[1, r]).astype(BF16)
        third(q).start()

    def finish(q):
        r = rows_of(q)
        second(q).wait()
        third(q).wait()
        summed[r] = (part[me, r] + rx1[0, r] + rx2[r].astype(F32)).astype(BF16)

    def fourth(q):
        r = rows_of(q)
        return remote(summed.at[r], rxs.at[r], ys.at[q], yr.at[q], (twin, me))

    def keys():
        return remote(key_ref, rxk, ks.at[0], ks.at[1], (twin, me))

    def send(d):
        return remote(pk.at[d], rxw.at[d], ws.at[d], wr.at[d], ((wide + 2 * d) % count, me))

    def dense(owner):
        places = lax.broadcasted_iota(I32, (height, summed.shape[0]), 0) + owner * height
        ours = (key_ref[...] == places).astype(F32).astype(BF16)
        theirs = (rxk[...] == places).astype(F32).astype(BF16)
        return jnp.dot(ours, summed[...], preferred_element_type=F32) + jnp.dot(
            theirs, rxs[...], preferred_element_type=F32
        )

    @pl.when(step == 0)
    def _():
        barrier = pltpu.get_barrier_semaphore()
        pl.semaphore_signal(barrier, inc=1, device_id=(wide, near), device_id_type=MESH)
        pl.semaphore_signal(barrier, inc=1, device_id=(wide, far), device_id_type=MESH)

        pl.semaphore_signal(barrier, inc=1, device_id=(twin, me), device_id_type=MESH)

        @pl.loop(1, half)
        def _(d):
            pl.semaphore_signal(
                barrier, inc=1, device_id=((wide + 2 * d) % count, me), device_id_type=MESH
            )

        pl.semaphore_wait(barrier, half + 2)
        keys().start()

    lane_half = lax.broadcasted_iota(I32, (1, 2 * HALF), 1) // HALF
    applied = []
    for j in range(ROWS):
        base = (step * ROWS + j) * terms
        for k in range(0, terms, 2):
            tiles = jnp.concatenate(
                [near_ref[tile_ref[base + k]], near_ref[tile_ref[base + k + 1]]], axis=1
            )
            stacked = op_ref[j, k : k + 2].reshape(-1, B)
            both = jnp.dot(stacked, tiles, preferred_element_type=F32)
            depth = both.shape[0] // 2
            applied.append(both[:depth, : 2 * HALF].astype(BF16))
            applied.append(both[depth:, 2 * HALF :].astype(BF16))
    rows = []
    for j in range(ROWS):
        base = (step * ROWS + j) * terms
        held = jnp.concatenate(applied[j * terms : (j + 1) * terms], axis=1)
        projected = jnp.dot(own_ref[j], held, preferred_element_type=F32)
        sums = [jnp.zeros((M, 2 * HALF), F32) for _ in range(KC // 2)]
        for k in range(terms):
            slot = slot_ref[base + k]
            piece = projected[:, k * 2 * HALF : (k + 1) * 2 * HALF]
            piece = jnp.where(swap_ref[base + k] == 1, pltpu.roll(piece, HALF, 1), piece)
            for t in range(KC // 2):
                sums[t] = sums[t] + jnp.where(lane_half + 2 * t == slot, piece, 0.0)
        rows.append(
            jnp.concatenate(
                [sums[s // 2][:, (s % 2) * HALF : (s % 2) * HALF + M] for s in range(KC)], axis=1
            )
        )
    block = QUAD * side
    for b in range(ROWS // QUAD):
        at = pl.ds(pl.multiple_of(step * (ROWS * side) + b * block, block), block)
        for g in range(parts):
            part[g, at] = jnp.concatenate(
                [row[g * side : (g + 1) * side] for row in rows[b * QUAD : (b + 1) * QUAD]], axis=0
            )

    @pl.when(step % per == per - 1)
    def _():
        first(step // per).start()
        second(step // per).start()

    @pl.when((step % per == per // 2) & (step >= per))
    def _():
        relay(step // per - 1)

    lag = 2

    @pl.when((step % per == per - 1) & (step >= lag * per))
    def _():
        finish(step // per - lag)
        fourth(step // per - lag).start()

    @pl.when(step == steps - 1)
    def _():
        relay(chunks - 1)
        for q in range(chunks - lag, chunks):
            finish(q)
            fourth(q).start()
        keys().wait()
        for q in range(chunks):
            fourth(q).wait()

        def turn(i):
            return 1 + (i + half // 2 - 1) % (half - 1)

        @pl.loop(0, half - 1)
        def _(i):
            d = turn(i)
            pk[d] = dense((wide + 2 * d) % count).astype(BF16)
            send(d).start()

        out_ref[...] = dense(wide)

        @pl.loop(0, half - 1)
        def _(i):
            d = turn(i)
            send(d).wait()
            out_ref[...] += rxw[d].astype(F32)


def coarse_rows(op_blocks, near, own, tiles, swaps, slots, keys, count, parts, chunks=8):
    count_rows, terms, part_rows, _ = op_blocks.shape
    side = M // parts
    height = AGG_DEV * side
    steps = count_rows // ROWS
    rows, columns = count_rows * side, KC * M
    vmem = pl.BlockSpec(memory_space=pltpu.VMEM)
    dma = pltpu.SemaphoreType.DMA
    return pl.pallas_call(
        functools.partial(coarse_kernel, count, parts, terms, steps, chunks),
        out_shape=jax.ShapeDtypeStruct((AGG_DEV * side, columns), F32),
        grid_spec=pltpu.PrefetchScalarGridSpec(
            num_scalar_prefetch=3,
            grid=(steps,),
            in_specs=[
                pl.BlockSpec((ROWS, terms, part_rows, B), lambda i, *_: (i, 0, 0, 0)),
                vmem,
                pl.BlockSpec((ROWS, M, part_rows), lambda i, *_: (i, 0, 0)),
                vmem,
            ],
            out_specs=pl.BlockSpec((AGG_DEV * side, columns), lambda i, *_: (0, 0)),
            scratch_shapes=[
                pltpu.VMEM((parts, rows, columns), F32),
                pltpu.VMEM((2, rows, columns), F32),
                pltpu.VMEM((rows, columns), BF16),
                pltpu.VMEM((rows, columns), BF16),
                pltpu.VMEM((count // 2, height, columns), BF16),
                pltpu.VMEM((count // 2, height, columns), BF16),
                pltpu.VMEM((1, rows), I32),
                pltpu.VMEM((rows, columns), BF16),
                pltpu.VMEM((rows, columns), BF16),
                dma((3, chunks)), dma((3, chunks)), dma((chunks,)), dma((chunks,)),
                dma((count // 2,)), dma((count // 2,)), dma((2,)),
            ],
        ),
        compiler_params=pltpu.CompilerParams(
            collective_id=0, has_side_effects=True, vmem_limit_bytes=48 << 20
        ),
    )(tiles, swaps, slots, op_blocks, near, own, keys)


def on_device(op_blocks, prolong, col_index, slot_index, dest_owner, dest_local):
    count_rows, _, part_rows, _ = op_blocks.shape
    count = lax.axis_size("wide")
    parts = lax.axis_size("narrow")
    wide_pos = lax.axis_index("wide")
    side = M // parts
    goal = (dest_owner[:, 0] * AGG_DEV + dest_local) * side
    keys = (goal[:, None] + jnp.arange(side, dtype=I32)[None, :]).reshape(1, -1)
    pairs = count_rows // 2
    blocks = prolong.reshape(count_rows, part_rows, M)
    gap = jnp.zeros((pairs, part_rows, HALF - M), BF16)
    paired = jnp.concatenate([blocks[:pairs], gap, blocks[pairs:], gap], axis=2)
    near = gathered(paired, count, parts)
    cols = (col_index - wide_pos * count_rows + count_rows).reshape(-1)
    slots = slot_index.reshape(-1)
    inner = cols % count_rows
    tiles = cols // count_rows * pairs + inner % pairs
    swaps = (inner // pairs + slots) % 2
    coarse = coarse_rows(
        op_blocks, near, blocks.swapaxes(1, 2), tiles, swaps, slots, keys, count, parts
    )
    return coarse.reshape(AGG_DEV, side, KC * M)


def solution(mesh):
    in_specs = (
        P("wide", None, "narrow", None),
        P("wide", "narrow"),
        P("wide", None),
        P("wide", None),
        P("wide", None),
        P("wide"),
    )
    out_specs = P("wide", "narrow", None)
    return jax.shard_map(
        on_device, mesh=mesh, in_specs=in_specs, out_specs=out_specs, check_vma=False
    )
```
